768 devices in a mesh: grp: 24 (over z, core), seg: 32 (over y, x).
Axes of the slice: x: 4, y: 8, z: 12, core: 2. Of those that a mesh axis runs over, the one named last changes fastest.
Arguments:
- initial_field: float32 [4, 96, 1024, 32], P(None, 'grp', 'seg'), may hold values from -6 to 6
- base_reluctivity: float32 [96, 1024, 32], P('grp', 'seg'), may hold values from 0.85 to 1
- saturation_rate: float32 [96, 1024, 32], P('grp', 'seg'), may hold values from 1 to 5
- mixing: float32 [4, 4], replicated, may hold values from -3 to 3
- face_contact: int32 [24, 256, 6], P('grp', 'seg'), may hold values 0 or 1
- new_owner: int32 [24, 256], P('grp', 'seg'), may hold values from 0 to 31, as said below
Outputs:
- new_blocks: float32 [24576, 4, 4, 128], P(('grp', 'seg'))
The draws below stay inside these ranges and needn't reach their ends.
Inputs may be any that keep to these rules, and one draw needn't show every extreme that they name: `new_owner`: of the blocks of one old owner, at most 1 go to the same new owner. In every group one new owner receives exactly 1 block from every old owner of the group, so exactly 32 blocks; the others receive fewer.
All inputs are finite; a program needn't handle non-finite values. No bound on the sum of `face_contact` on one device may be relied on, other than what follows from the above.
Results may differ from the reference program's by a relative error of at most 0.00007.
Values sent between devices are 32-bit elements; how exact they have to be, the bound alone decides.
No kernel may reach another device: no remote copies, remote signals or barrier semaphores. Data moves between devices by JAX's collectives and lax.ppermute only.
A program may use at most 32 MiB of HBM per device.

```python
import math
import jax
import jax.numpy as jnp

BXC = 4
BYC = 16
BZC = 8
BLY = 2
BLZ = 4
SLOT = 1
STEPS1 = 4
STEPS2 = 4
BLK_DEV = 8
NX = 96
NY = 1024
NZ = 32
N_GRP = 24
N_SEG = 32


def draw_new_owner(key, part):

    def one_group(group_key):
        heavy_key, source_key = jax.random.split(group_key)
        heavy = jax.random.randint(heavy_key, (), 0, N_SEG)
        others = (heavy + 1 + jnp.arange(N_SEG - 1)) % N_SEG
        choices_pool = jnp.tile(others, SLOT)

        def one_source(sender_key):
            pick_key, order_key = jax.random.split(sender_key)
            picked = jax.random.permutation(pick_key, choices_pool)[:BLK_DEV - SLOT]
            targets = jnp.concatenate([jnp.full((SLOT,), heavy, dtype=picked.dtype), picked])
            return jax.random.permutation(order_key, targets)
        return jax.vmap(one_source)(jax.random.split(source_key, N_SEG)).reshape(-1)
    return jax.vmap(one_group)(jax.random.split(key, N_GRP)).astype(jnp.int32)


def set_ends(drawn, rng, smallest, top_value):
    longest = drawn.shape.index(max(drawn.shape))
    spots = []
    for shift in (0, 1):
        where = [jax.random.randint(jax.random.fold_in(rng, axis), (), 0, length) for axis, length in enumerate(drawn.shape)]
        where[longest] = (where[longest] + shift) % drawn.shape[longest]
        spots.append(tuple(where))
    return drawn.at[spots[0]].set(smallest).at[spots[1]].set(top_value)


def block_levels(stream_key, dims, cuts, least, high):
    gain, own = 1.0, jax.random.fold_in(stream_key, 6)
    for position, shards_of in cuts:
        draws = jnp.exp(jax.random.uniform(jax.random.fold_in(own, position), (shards_of,), jnp.float32, least / len(cuts), high / len(cuts)))
        gain = gain * jnp.repeat(draws, dims[position] // shards_of).reshape([-1 if axis == position else 1 for axis in range(len(dims))])
    return gain


def noise(stream_key, shape, width, limit, shards=(), kind=jnp.bfloat16):
    entries = jax.random.normal(stream_key, shape, jnp.float32) * width
    if len(shards) > 0:
        entries = block_levels(stream_key, shape, shards, -0.22, 0.18) * entries
    return jnp.clip(entries, min=-limit, max=limit).astype(kind)


def setup_inputs(seed: int = 0) -> dict:
    arg_keys = jax.random.split(jax.random.key(seed), 7)
    return {
        "initial_field": noise(arg_keys[0], (4, NX, NY, NZ), 1.0, 6.0, ((1, 24), (2, 32)), jnp.float32),
        "base_reluctivity": jnp.clip(jnp.exp(math.log(1.0) - 0.1625189 * jax.random.uniform(arg_keys[1], (NX, NY, NZ), jnp.float32) ** block_levels(arg_keys[1], (NX, NY, NZ), ((0, 24), (1, 32)), -0.2, 0.2)), 0.85, 1.0),
        "saturation_rate": jnp.clip(jnp.exp(math.log(5.0) - 1.609438 * jax.random.uniform(arg_keys[2], (NX, NY, NZ), jnp.float32) ** block_levels(arg_keys[2], (NX, NY, NZ), ((0, 24), (1, 32)), -0.2, 0.2)), 1.0, 5.0),
        "mixing": noise(arg_keys[3], (4, 4), 0.7, 3.0, (), jnp.float32),
        "face_contact": set_ends((jax.random.randint(arg_keys[4], (N_GRP, N_SEG * BLK_DEV, 6), 0, 4) < 3).astype(jnp.int32), jax.random.fold_in(arg_keys[4], 1), 0, 1),
        "new_owner": draw_new_owner(jax.random.fold_in(arg_keys[6], 71), 0),
    }


step_size = 0.05


def advance(components, neighbours, coefficients, base_reluctivity, saturation_rate, mixing):
    differences = [[coefficients[direction] * (neighbours[direction][channel] - components[channel]) for channel in range(4)] for direction in range(6)]
    field_x = differences[3][2] - differences[5][1]
    field_y = differences[5][0] - differences[1][2]
    field_z = differences[1][1] - differences[3][0]
    saturation = saturation_rate * (field_x * field_x + field_y * field_y + field_z * field_z)
    reluctivity = base_reluctivity * (1.0 + 2.0 * saturation / (1.0 + saturation))
    updated = []
    for channel in range(4):
        laplacian = differences[0][channel]
        for direction in range(1, 6):
            laplacian = laplacian + differences[direction][channel]
        coupled = mixing[channel, 0] * components[0]
        for source_channel in range(1, 4):
            coupled = coupled + mixing[channel, source_channel] * components[source_channel]
        updated.append(components[channel] + step_size * (reluctivity * laplacian + coupled))
    return updated


def slab_coefficients(grid):
    blocks_x, blocks_y, blocks_z = grid.shape[0], grid.shape[1], grid.shape[2]
    position_x = (jnp.arange(blocks_x * BXC) % BXC)[:, None, None]
    position_y = (jnp.arange(blocks_y * BYC) % BYC)[None, :, None]
    position_z = (jnp.arange(blocks_z * BZC) % BZC)[None, None, :]
    edge_cells = [position_x == 0, position_x == BXC - 1, position_y == 0, position_y == BYC - 1, position_z == 0, position_z == BZC - 1]
    result = []
    for direction in range(6):
        spread = grid[:, :, :, direction].astype(jnp.float32)
        spread = jnp.repeat(jnp.repeat(jnp.repeat(spread, BXC, axis=0), BYC, axis=1), BZC, axis=2)
        result.append(jnp.where(edge_cells[direction], spread, jnp.ones_like(spread)))
    return result


def slab_step(state, padded, coefficients, base_reluctivity, saturation_rate, mixing):
    neighbours = [padded[:, :-2, 1:-1, 1:-1], padded[:, 2:, 1:-1, 1:-1], padded[:, 1:-1, :-2, 1:-1], padded[:, 1:-1, 2:, 1:-1], padded[:, 1:-1, 1:-1, :-2], padded[:, 1:-1, 1:-1, 2:]]
    return jnp.stack(advance(state, neighbours, coefficients, base_reluctivity, saturation_rate, mixing))


def block_coefficients():
    position_x = jnp.arange(BXC)[:, None]
    merged = jnp.arange(BYC * BZC)[None, :]
    position_y = merged // BZC
    position_z = merged % BZC
    tests = [position_x > 0, position_x < BXC - 1, position_y > 0, position_y < BYC - 1, position_z > 0, position_z < BZC - 1]
    return [jnp.where(test, 1.0, 0.0).astype(jnp.float32) for test in tests]


def block_steps(blocks, material, mixing):
    state = jnp.moveaxis(blocks, 1, 0)
    properties = jnp.moveaxis(material, 1, 0)
    coefficients = block_coefficients()
    for sweep in range(STEPS2):
        neighbours = [jnp.roll(state, 1, 2), jnp.roll(state, -1, 2), jnp.roll(state, BZC, 3), jnp.roll(state, -BZC, 3), jnp.roll(state, 1, 3), jnp.roll(state, -1, 3)]
        state = jnp.stack(advance(state, neighbours, coefficients, properties[0], properties[1], mixing))
    return jnp.moveaxis(state, 0, 1)


def to_blocks(array):
    channels = array.shape[0]
    blocks_x = array.shape[1] // BXC
    blocks_y = array.shape[2] // BYC
    blocks_z = array.shape[3] // BZC
    shaped = array.reshape(channels, blocks_x, BXC, blocks_y, BYC, blocks_z, BZC)
    shaped = shaped.transpose(1, 3, 5, 0, 2, 4, 6)
    return shaped.reshape(blocks_x * blocks_y * blocks_z, channels, BXC, BYC * BZC)


def slot_rank(owners):
    count = owners.shape[-1]
    same = owners[..., :, None] == owners[..., None, :]
    earlier = jnp.arange(count)[None, :] < jnp.arange(count)[:, None]
    return jnp.sum(jnp.logical_and(same, earlier), axis=-1).astype(jnp.int32)


def reference(initial_field, base_reluctivity, saturation_rate, mixing, face_contact, new_owner):
    coefficients = slab_coefficients(face_contact.reshape(N_GRP, N_SEG * BLY, BLZ, 6))
    state = initial_field
    for sweep in range(STEPS1):
        padded = jnp.pad(state, ((0, 0), (1, 1), (1, 1), (1, 1)))
        state = slab_step(state, padded, coefficients, base_reluctivity, saturation_rate, mixing)
    blocks = to_blocks(state)
    material = to_blocks(jnp.stack([base_reluctivity, saturation_rate]))
    settled = block_steps(blocks, material, mixing)
    owners = new_owner.reshape(N_GRP, N_SEG, BLK_DEV)
    ranks = slot_rank(owners)
    sources = jnp.arange(N_SEG).astype(jnp.int32)[None, :, None]
    target = owners * (N_SEG * SLOT) + sources * SLOT + ranks
    output = jnp.zeros((N_GRP, N_SEG * N_SEG * SLOT, 4, BXC, BYC * BZC), jnp.float32)
    groups = jnp.arange(N_GRP).astype(jnp.int32)[:, None]
    output = output.at[groups, target.reshape(N_GRP, N_SEG * BLK_DEV)].set(settled.reshape(N_GRP, N_SEG * BLK_DEV, 4, BXC, BYC * BZC))
    return output.reshape(N_GRP * N_SEG * N_SEG * SLOT, 4, BXC, BYC * BZC)
```

```python
import jax
import jax.numpy as jnp
from jax import lax
from jax.experimental import pallas as pl
from jax.experimental.pallas import tpu as pltpu
from jax.sharding import PartitionSpec as P

BXC = 4
BYC = 16
BZC = 8
BLY = 2
BLZ = 4
STEPS1 = 4
STEPS2 = 4
ROWS = BLY * BLZ
LANES = BYC * BZC
CH = 6
SLABS = CH * BXC
FC = SLABS * ROWS
HFC = FC + ROWS
LOW = HFC + ROWS
HIGH = LOW + SLABS
PACK = HIGH + SLABS
EXT = 3 * BXC
step_size = 0.05

VMEM = pl.BlockSpec(memory_space=pltpu.VMEM)
SMEM = pl.BlockSpec(memory_space=pltpu.SMEM)


def iotas():
    row = lax.broadcasted_iota(jnp.int32, (ROWS, LANES), 0)
    lane = lax.broadcasted_iota(jnp.int32, (ROWS, LANES), 1)
    return row, lane


def lanes_of(rows):
    return lax.broadcasted_iota(jnp.int32, (rows, LANES), 1)


def lroll(value, shift):
    return value if shift % LANES == 0 else pltpu.roll(value, shift % LANES, 1)


def sroll(value, shift):
    return pltpu.roll(value, shift % ROWS, 0)


def pack_kernel(field_ref, base_ref, rate_ref, contact_ref, own_ref, up_ref, down_ref, wide):
    cells = BLY * BYC
    parts = ((field_ref, 0, 4 * BXC), (base_ref, 4 * BXC, BXC), (rate_ref, 5 * BXC, BXC))
    wide[...] = jnp.zeros_like(wide)
    for ref, first, count in parts:
        wide[pl.ds(first * cells, count * cells), 0 : BLZ * BZC] = ref[...]
    count = SLABS * BLY
    group = lanes_of(count) // BZC
    placed = [None] * BLZ
    for yi in range(BYC):
        value = wide[pl.ds(yi, count, stride=BYC), :]
        for kz in range(BLZ):
            moved = lroll(value, BZC * (yi - kz))
            placed[kz] = moved if yi == 0 else jnp.where(group == yi, moved, placed[kz])
    for kz in range(BLZ):
        own_ref[pl.ds(kz, count, stride=BLZ), :] = placed[kz]
    contact = jnp.zeros((ROWS, LANES), jnp.float32)
    own_ref[pl.ds(FC, ROWS), :] = contact
    own_ref[pl.ds(FC, ROWS), 0:6] = contact_ref[...].astype(jnp.float32)
    quarter = lanes_of(SLABS) // (LANES // 4)
    for ref, jy, start in ((up_ref, BLY - 1, LANES - LANES // 4), (down_ref, 0, 0)):
        edge = None
        for kz in range(BLZ):
            value = own_ref[pl.ds(jy * BLZ + kz, SLABS, stride=ROWS), :]
            moved = lroll(value, kz * (LANES // 4) - start)
            edge = moved if kz == 0 else jnp.where(quarter == kz, moved, edge)
        ref[pl.ds(0, SLABS), :] = edge
        ref[pl.ds(SLABS, ROWS), :] = own_ref[pl.ds(FC, ROWS), :]


def join_kernel(own_ref, below_ref, above_ref, out_ref):
    row, _ = iotas()
    out_ref[pl.ds(0, HFC), :] = own_ref[...]
    below = sroll(below_ref[pl.ds(SLABS, ROWS), :], 4)
    above = sroll(above_ref[pl.ds(SLABS, ROWS), :], 4)
    out_ref[pl.ds(HFC, ROWS), :] = jnp.where(row < 4, below, above)
    out_ref[pl.ds(LOW, SLABS), :] = below_ref[pl.ds(0, SLABS), :]
    out_ref[pl.ds(HIGH, SLABS), :] = above_ref[pl.ds(0, SLABS), :]


def slot(i, channel):
    return (i // BXC) * SLABS + channel * BXC + i % BXC


def relax(differences, laplacian, values, base, rate, mix):
    e_xh, e_yh, e_zh = differences
    field_x = e_yh[2] - e_zh[1]
    field_y = e_zh[0] - e_xh[2]
    field_z = e_xh[1] - e_yh[0]
    saturation = rate * (field_x * field_x + field_y * field_y + field_z * field_z)
    reluctivity = base * (3.0 - 2.0 / (1.0 + saturation))
    updated = []
    for channel in range(4):
        total = reluctivity * laplacian[channel]
        for source in range(4):
            total = total + mix[channel][source] * values[source]
        updated.append(total)
    return updated


def update_kernel(
    mix_ref, owner_ref, own_ref, low_ref, high_ref, out_ref, inner, outer, cin, cout, done
):
    row, lane = iotas()
    kz, yi, zi = row % BLZ, lane // BZC, lane % BZC
    first_half = row < BLZ
    mix = [
        [step_size * mix_ref[c, e] + (1.0 if c == e else 0.0) for e in range(4)] for c in range(4)
    ]
    one = jnp.ones((ROWS, LANES), jnp.float32)

    for part, ref in enumerate((low_ref, own_ref, high_ref)):
        inner[0, pl.ds(part * FC, FC), :] = ref[pl.ds(0, FC), :]
        compact_low = ref[pl.ds(LOW, SLABS), :]
        compact_high = ref[pl.ds(HIGH, SLABS), :]
        wide_lane = lanes_of(SLABS)
        for k in range(BLZ):
            below = lroll(compact_low, LANES - (k + 1) * (LANES // 4))
            above = lroll(compact_high, -k * (LANES // 4))
            value = jnp.where(
                wide_lane < LANES // 4, above, jnp.where(wide_lane >= LANES - LANES // 4, below, 0.0)
            )
            outer[0, pl.ds(part * FC + k, SLABS, stride=ROWS), :] = value
            outer[0, pl.ds(part * FC + k + BLZ, SLABS, stride=ROWS), :] = value
        contact = ref[pl.ds(FC, ROWS), :]
        beside = ref[pl.ds(HFC, ROWS), :]
        turned = sroll(beside, BLZ)
        below = jnp.where(first_half, beside, turned)
        above = jnp.where(first_half, turned, beside)
        spread = lambda tile, d: jnp.broadcast_to(tile[:, d : d + 1], (ROWS, LANES))
        faces_in = [spread(contact, d) for d in range(6)]
        faces_out = [
            jnp.where(lane < LANES // 2, spread(above, d), spread(below, d)) for d in range(6)
        ]
        for coefficients, faces in ((cin, faces_in), (cout, faces_out)):
            ylow = jnp.where(yi == 0, faces[2], one)
            yhigh = jnp.where(yi == BYC - 1, faces[3], one)
            zlow = jnp.where(zi == 0, faces[4], one)
            zlow_n = jnp.where(jnp.logical_and(zi == 0, kz == 0), 0.0, zlow)
            zhigh = jnp.where(zi == BZC - 1, faces[5], one)
            zhigh_n = jnp.where(jnp.logical_and(zi == BZC - 1, kz == BLZ - 1), 0.0, zhigh)
            for x in range(BXC):
                xlow = faces[0] if x == 0 else one
                xhigh = faces[1] if x == BXC - 1 else one
                entries = (xlow, xhigh, ylow, yhigh, zlow_n, zhigh, zhigh_n, xlow + ylow + zlow)
                for d, entry in enumerate(entries):
                    coefficients[part * BXC + x, d] = entry

    def tile(ref, which, i, channel):
        at = pl.multiple_of(slot(i, channel) * ROWS, ROWS)
        return ref[which, pl.ds(at, ROWS), :]

    def sweep(now, i, with_outer):
        refs = (inner, outer) if with_outer else (inner,)
        coefs = (cin, cout)
        laps = [[], []]
        diffs = [([], [], []), ([], [], [])]
        values = [[], []]
        loaded = [
            [[cf[i, d] for d in range(8)] for cf in coefs[: len(refs)]],
        ][0]
        for c in range(4):
            u = tile(inner, now, i, c)
            h = tile(outer, now, i, c)
            u_up, h_up = lroll(u, -BZC), lroll(h, -BZC)
            u_down, h_down = lroll(u, BZC), lroll(h, BZC)
            turn_up, turn_down = sroll(u_up, BLZ), sroll(u_down, BLZ)
            here = [(u, u_up, u_down)] + ([(h, h_up, h_down)] if with_outer else [])
            over_up = [jnp.where(first_half, turn_up, h_up), jnp.where(first_half, u_up, turn_up)]
            over_down = [
                jnp.where(first_half, h_down, turn_down),
                jnp.where(first_half, turn_down, u_down),
            ]
            for part, (v, v_up, v_down) in enumerate(here):
                ref = refs[part]
                cxl, cxh, cyl, cyh, nzl, czh, nzh, low = loaded[part]
                n_yh = jnp.where(yi < BYC - 1, v_up, over_up[part])
                n_yl = jnp.where(yi > 0, v_down, over_down[part])
                n_zh = jnp.where(zi < BZC - 1, lroll(v, -1), sroll(lroll(v, BZC - 1), -1))
                n_zl = jnp.where(zi > 0, lroll(v, 1), sroll(lroll(v, 1 - BZC), 1))
                n_xl = tile(ref, now, i - 1, c)
                n_xh = tile(ref, now, i + 1, c)
                e_xh = cxh * (n_xh - v)
                e_yh = cyh * (n_yh - v)
                e_zh = nzh * n_zh - czh * v
                lap = cxl * n_xl + cyl * n_yl + nzl * n_zl - low * v
                laps[part].append(lap + (e_xh + e_yh + e_zh))
                diffs[part][0].append(e_xh)
                diffs[part][1].append(e_yh)
                diffs[part][2].append(e_zh)
                values[part].append(v)
        for part, ref in enumerate(refs):
            base = tile(ref, 0, i, 4) * step_size
            rate = tile(ref, 0, i, 5)
            updated = relax(diffs[part], laps[part], values[part], base, rate, mix)
            for c in range(4):
                at = pl.multiple_of(slot(i, c) * ROWS, ROWS)
                ref[1 - now, pl.ds(at, ROWS), :] = updated[c]

    for step in range(STEPS1):
        last = step == STEPS1 - 1

        def layer(i, carry, now=step % 2, with_outer=not last):
            sweep(now, i, with_outer)
            return carry

        lax.fori_loop(step + 1, EXT - 1 - step, layer, 0)

    y_inner = jnp.where(yi < BYC - 1, 1.0, 0.0)
    z_inner = jnp.where(zi < BZC - 1, 1.0, 0.0)
    y_low_inner = jnp.where(yi > 0, 1.0, 0.0)
    z_low_inner = jnp.where(zi > 0, 1.0, 0.0)
    out_ref[...] = jnp.zeros_like(out_ref)
    start = STEPS1 % 2
    state = [[tile(inner, start, BXC + x, c) for c in range(4)] for x in range(BXC)]
    for step in range(STEPS2):
        fresh = []
        rise = [
            [state[x + 1][c] - state[x][c] for c in range(4)] for x in range(BXC - 1)
        ]
        for x in range(BXC):
            laps, diffs = [], ([], [], [])
            for c in range(4):
                v = state[x][c]
                e_yh = y_inner * (lroll(v, -BZC) - v)
                e_zh = z_inner * (lroll(v, -1) - v)
                e_yl = y_low_inner * (lroll(v, BZC) - v)
                e_zl = z_low_inner * (lroll(v, 1) - v)
                lap = (e_yl + e_yh) + (e_zl + e_zh)
                if x < BXC - 1:
                    lap = lap + rise[x][c]
                if x > 0:
                    lap = lap - rise[x - 1][c]
                laps.append(lap)
                diffs[0].append(rise[x][c] if x < BXC - 1 else jnp.zeros_like(v))
                diffs[1].append(e_yh)
                diffs[2].append(e_zh)
            base = tile(inner, 0, BXC + x, 4) * step_size
            rate = tile(inner, 0, BXC + x, 5)
            fresh.append(relax(diffs, laps, state[x], base, rate, mix))
        state = fresh
    for x in range(BXC):
        for c in range(4):
            done[pl.ds((c * BXC + x) * ROWS, ROWS), :] = state[x][c]
    for block in range(ROWS):
        out_ref[owner_ref[0, block]] = done[pl.ds(block, 4 * BXC, stride=ROWS), :]


def on_device(initial_field, base_reluctivity, saturation_rate, mixing, face_contact, new_owner):
    f32 = jnp.float32
    cells = BLY * BYC
    peers = lax.axis_size("seg")
    own, up, down = pl.pallas_call(
        pack_kernel,
        out_shape=(
            jax.ShapeDtypeStruct((HFC, LANES), f32),
            jax.ShapeDtypeStruct((SLABS + ROWS, LANES), f32),
            jax.ShapeDtypeStruct((SLABS + ROWS, LANES), f32),
        ),
        in_specs=[VMEM] * 4,
        out_specs=(VMEM, VMEM, VMEM),
        scratch_shapes=[pltpu.VMEM((SLABS * cells, LANES), f32)],
        name="pack",
    )(
        initial_field.reshape(4 * BXC * cells, BLZ * BZC),
        base_reluctivity.reshape(BXC * cells, BLZ * BZC),
        saturation_rate.reshape(BXC * cells, BLZ * BZC),
        face_contact[0],
    )

    def both_ways(to_next, to_last, axis):
        size = lax.axis_size(axis)
        rising = [(i, i + 1) for i in range(size - 1)]
        falling = [(j, i) for i, j in rising]
        return lax.ppermute(to_next, axis, rising), lax.ppermute(to_last, axis, falling)

    below, above = both_ways(up, down, "seg")
    package = pl.pallas_call(
        join_kernel,
        out_shape=jax.ShapeDtypeStruct((PACK, LANES), f32),
        in_specs=[VMEM] * 3,
        out_specs=VMEM,
        name="join",
    )(own, below, above)
    low, high = both_ways(package, package, "grp")
    placed = pl.pallas_call(
        update_kernel,
        out_shape=jax.ShapeDtypeStruct((peers, 4 * BXC, LANES), f32),
        in_specs=[SMEM, SMEM, VMEM, VMEM, VMEM],
        out_specs=VMEM,
        scratch_shapes=[
            pltpu.VMEM((2, 3 * FC, LANES), f32),
            pltpu.VMEM((2, 3 * FC, LANES), f32),
            pltpu.VMEM((EXT, 8, ROWS, LANES), f32),
            pltpu.VMEM((EXT, 8, ROWS, LANES), f32),
            pltpu.VMEM((4 * BXC * ROWS, LANES), f32),
        ],
        name="update",
    )(mixing, new_owner, package, low, high)
    received = lax.all_to_all(placed, "seg", split_axis=0, concat_axis=0, tiled=True)
    return received.reshape(peers, 4, BXC, LANES)


def solution(mesh):
    return jax.shard_map(
        on_device,
        mesh=mesh,
        in_specs=(
            P(None, "grp", "seg", None),
            P("grp", "seg", None),
            P("grp", "seg", None),
            P(),
            P("grp", "seg", None),
            P("grp", "seg"),
        ),
        out_specs=P(("grp", "seg"), None, None, None),
        check_vma=False,
    )
```

```python
import jax
import jax.numpy as jnp
from jax import lax
from jax.experimental import pallas as pl
from jax.experimental.pallas import tpu as pltpu
from jax.sharding import PartitionSpec as P

BXC = 4
BYC = 16
BZC = 8
BLY = 2
BLZ = 4
STEPS1 = 4
STEPS2 = 4
ROWS = BLY * BLZ
LANES = BYC * BZC
CH = 6
SLABS = CH * BXC
FC = SLABS * ROWS
HFC = FC + ROWS
LOW = HFC + ROWS
HIGH = LOW + SLABS
PACK = HIGH + SLABS
EXT = 3 * BXC
step_size = 0.05

VMEM = pl.BlockSpec(memory_space=pltpu.VMEM)
SMEM = pl.BlockSpec(memory_space=pltpu.SMEM)


def iotas():
    row = lax.broadcasted_iota(jnp.int32, (ROWS, LANES), 0)
    lane = lax.broadcasted_iota(jnp.int32, (ROWS, LANES), 1)
    return row, lane


def lanes_of(rows):
    return lax.broadcasted_iota(jnp.int32, (rows, LANES), 1)


def lroll(value, shift):
    return value if shift % LANES == 0 else pltpu.roll(value, shift % LANES, 1)


def sroll(value, shift):
    return pltpu.roll(value, shift % ROWS, 0)


def pack_kernel(field_ref, base_ref, rate_ref, contact_ref, own_ref, up_ref, down_ref):
    first = 0
    for ref, slabs in ((field_ref, 4 * BXC), (base_ref, BXC), (rate_ref, BXC)):
        count = slabs * BLY
        group = lanes_of(count) // BZC % BLZ
        placed = [None] * BLZ
        for q in range(BLZ):
            mixed = jnp.concatenate(
                [ref[pl.ds(BLZ * r + q, count, stride=BYC), :] for r in range(BLZ)], axis=1
            )
            for kz in range(BLZ):
                moved = lroll(mixed, BZC * (q - kz))
                placed[kz] = moved if q == 0 else jnp.where(group == q, moved, placed[kz])
        for kz in range(BLZ):
            own_ref[pl.ds(first * ROWS + kz, count, stride=BLZ), :] = placed[kz]
        first += slabs
    row, lane = iotas()
    contact = jnp.zeros((ROWS, LANES), jnp.float32)
    for d in range(6):
        for block in range(ROWS):
            here = jnp.logical_and(row == block, lane == d)
            contact = jnp.where(here, contact_ref[d, block].astype(jnp.float32), contact)
    own_ref[pl.ds(FC, ROWS), :] = contact
    quarter = lanes_of(SLABS) // (LANES // 4)
    for ref, jy, start in ((up_ref, BLY - 1, LANES - LANES // 4), (down_ref, 0, 0)):
        edge = None
        for kz in range(BLZ):
            value = own_ref[pl.ds(jy * BLZ + kz, SLABS, stride=ROWS), :]
            moved = lroll(value, kz * (LANES // 4) - start)
            edge = moved if kz == 0 else jnp.where(quarter == kz, moved, edge)
        ref[pl.ds(0, SLABS), :] = edge
        ref[pl.ds(SLABS, ROWS), :] = contact


def join_kernel(own_ref, below_ref, above_ref, out_ref):
    row, _ = iotas()
    out_ref[pl.ds(0, HFC), :] = own_ref[...]
    below = sroll(below_ref[pl.ds(SLABS, ROWS), :], 4)
    above = sroll(above_ref[pl.ds(SLABS, ROWS), :], 4)
    out_ref[pl.ds(HFC, ROWS), :] = jnp.where(row < 4, below, above)
    out_ref[pl.ds(LOW, SLABS), :] = below_ref[pl.ds(0, SLABS), :]
    out_ref[pl.ds(HIGH, SLABS), :] = above_ref[pl.ds(0, SLABS), :]


def relax(differences, laplacian, values, base, rate, mix):
    e_xh, e_yh, e_zh = differences
    field_x = e_yh[2] - e_zh[1]
    field_y = e_zh[0] - e_xh[2]
    field_z = e_xh[1] - e_yh[0]
    saturation = rate * (field_x * field_x + field_y * field_y + field_z * field_z)
    reluctivity = base * (3.0 - 2.0 / (1.0 + saturation))
    updated = []
    for channel in range(4):
        total = reluctivity * laplacian[channel]
        for source in range(4):
            total = total + mix[channel][source] * values[source]
        updated.append(total)
    return updated


RING = 2 * ROWS
PAD = ROWS


def update_kernel(mix_ref, owner_ref, own_ref, low_ref, high_ref, out_ref, *scratch):
    ring, cin, done = scratch
    row, lane = iotas()
    kz, yi, zi = row % BLZ, lane // BZC, lane % BZC
    first_half = row < BLZ
    mix = [
        [step_size * mix_ref[c, e] + (1.0 if c == e else 0.0) for e in range(4)] for c in range(4)
    ]
    one = jnp.ones((ROWS, LANES), jnp.float32)
    zero = jnp.zeros((ROWS, LANES), jnp.float32)
    total = EXT * CH * RING

    def at(i, channel):
        return PAD + (i // BXC * SLABS + channel * BXC + i % BXC) * RING

    for now in range(2):
        ring[now, pl.ds(0, PAD), :] = zero
        ring[now, pl.ds(PAD + total, PAD), :] = zero
    for i, channel in ((0, 1), (0, 2), (0, 3), (0, 4), (BXC, 4)):
        ring[1, pl.ds(at(i, channel), ROWS), :] = zero
    for i, channel in ((BXC - 1, 5), (2 * BXC - 1, 5), (EXT - 1, 0), (EXT - 1, 1), (EXT - 1, 2)):
        ring[1, pl.ds(at(i, channel) + ROWS, ROWS), :] = zero
    faces = []
    for part, ref in enumerate((low_ref, own_ref, high_ref)):
        begin = PAD + part * SLABS * RING
        for slab in range(SLABS):
            ring[0, pl.ds(begin + slab * RING + BLZ, ROWS), :] = ref[pl.ds(slab * ROWS, ROWS), :]
        compact_low = ref[pl.ds(LOW, SLABS), :]
        compact_high = ref[pl.ds(HIGH, SLABS), :]
        wide_lane = lanes_of(SLABS)
        for k in range(BLZ):
            below = lroll(compact_low, LANES - (k + 1) * (LANES // 4))
            above = lroll(compact_high, -k * (LANES // 4))
            beyond = jnp.where(wide_lane >= LANES - LANES // 4, below, 0.0)
            beyond = jnp.where(wide_lane < LANES // 4, above, beyond)
            ring[0, pl.ds(begin + k, SLABS, stride=RING), :] = beyond
            ring[0, pl.ds(begin + k + 3 * BLZ, SLABS, stride=RING), :] = beyond
        contact = ref[pl.ds(FC, ROWS), :]
        beside = ref[pl.ds(HFC, ROWS), :]
        for d in range(6):
            ab = jnp.broadcast_to(contact[:, d : d + 1], (ROWS, LANES))
            ba = sroll(ab, BLZ)
            owners = jnp.broadcast_to(beside[:, d : d + 1], (ROWS, LANES))
            c = jnp.where(lane < LANES // 2, sroll(owners, BLZ), owners)
            ca = jnp.where(first_half, c, ba)
            bc = jnp.where(first_half, ba, sroll(c, BLZ))
            faces.append((ca, bc, ab))
    for part in range(3):
        for g in range(3):
            f = [faces[part * 6 + d][g] for d in range(6)]
            ylow = jnp.where(yi == 0, f[2], one)
            yhigh = jnp.where(yi == BYC - 1, f[3], one)
            zlow = jnp.where(zi == 0, f[4], one)
            zlow_n = jnp.where(jnp.logical_and(zi == 0, kz == 0), 0.0, zlow)
            zhigh = jnp.where(zi == BZC - 1, f[5], one)
            zhigh_n = jnp.where(jnp.logical_and(zi == BZC - 1, kz == BLZ - 1), 0.0, zhigh)
            entries = (ylow, yhigh, zlow_n, zhigh, zhigh_n, ylow + zlow, f[0], f[1])
            for d, entry in enumerate(entries):
                cin[part, g, d] = entry

    def put(now, start, value):
        ring[now, pl.ds(start, ROWS), :] = value

    def sweep(now, i, last):
        part, x = i // BXC, i % BXC
        groups = (2,) if last else (0, 1)
        offset = {0: 0, 1: ROWS, 2: BLZ}
        coefs = {g: [cin[part, g, d] for d in range(8)] for g in groups}
        laps = {g: [] for g in groups}
        diffs = {g: ([], [], []) for g in groups}
        values = {g: [] for g in groups}
        for c in range(4):
            start, before, after = at(i, c), at(i - 1, c), at(i + 1, c)

            def tile(begin):
                return ring[now, pl.ds(begin, ROWS), :]

            rows = [tile(start + offset[g]) for g in range(3)]
            following, previous = {0: 2, 1: 0, 2: 1}, {0: 1, 1: 2, 2: 0}
            ups = [lroll(v, -BZC) for v in rows]
            downs = [lroll(v, BZC) for v in rows]
            for g in groups:
                v = rows[g]
                cyl, cyh, nzl, czh, nzh, low, cxl, cxh = coefs[g]
                n_yh = jnp.where(yi < BYC - 1, ups[g], ups[following[g]])
                n_yl = jnp.where(yi > 0, downs[g], downs[previous[g]])
                z_next = lroll(tile(start + offset[g] + 1), BZC - 1)
                z_last = lroll(tile(start + offset[g] - 1), 1 - BZC)
                n_zh = jnp.where(zi < BZC - 1, lroll(v, -1), z_next)
                n_zl = jnp.where(zi > 0, lroll(v, 1), z_last)
                e_xl = v - tile(before + offset[g])
                if x == 0:
                    e_xl = cxl * e_xl
                e_xh = tile(after + offset[g]) - v
                if x == BXC - 1:
                    e_xh = cxh * e_xh
                e_yh = cyh * (n_yh - v)
                e_zh = nzh * n_zh - czh * v
                lap = (cyl * n_yl + nzl * n_zl) - low * v
                laps[g].append((lap - e_xl) + (e_xh + (e_yh + e_zh)))
                diffs[g][0].append(e_xh)
                diffs[g][1].append(e_yh)
                diffs[g][2].append(e_zh)
                values[g].append(v)
        for g in groups:
            base = ring[0, pl.ds(at(i, 4) + offset[g], ROWS), :] * step_size
            rate = ring[0, pl.ds(at(i, 5) + offset[g], ROWS), :]
            updated = relax(diffs[g], laps[g], values[g], base, rate, mix)
            if last:
                state[x] = updated
            else:
                for c in range(4):
                    put(1 - now, at(i, c) + offset[g], updated[c])

    state = [None] * BXC
    for step in range(STEPS1):
        for i in range(step + 1, EXT - 1 - step):
            sweep(step % 2, i, step == STEPS1 - 1)

    y_inner = jnp.where(yi < BYC - 1, 1.0, 0.0)
    z_inner = jnp.where(zi < BZC - 1, 1.0, 0.0)
    y_low_inner = jnp.where(yi > 0, 1.0, 0.0)
    z_low_inner = jnp.where(zi > 0, 1.0, 0.0)
    out_ref[...] = jnp.zeros_like(out_ref)
    for step in range(STEPS2):
        fresh = []
        rise = [[state[x + 1][c] - state[x][c] for c in range(4)] for x in range(BXC - 1)]
        rise.append([zero] * 4)
        for x in range(BXC):
            laps, diffs = [], ([], [], [])
            for c in range(4):
                v = state[x][c]
                e_yh = y_inner * (lroll(v, -BZC) - v)
                e_zh = z_inner * (lroll(v, -1) - v)
                e_yl = y_low_inner * (lroll(v, BZC) - v)
                e_zl = z_low_inner * (lroll(v, 1) - v)
                lap = (e_yl + e_yh) + (e_zl + e_zh)
                if x < BXC - 1:
                    lap = lap + rise[x][c]
                if x > 0:
                    lap = lap - rise[x - 1][c]
                laps.append(lap)
                diffs[0].append(rise[x][c])
                diffs[1].append(e_yh)
                diffs[2].append(e_zh)
            base = ring[0, pl.ds(at(BXC + x, 4) + BLZ, ROWS), :] * step_size
            rate = ring[0, pl.ds(at(BXC + x, 5) + BLZ, ROWS), :]
            fresh.append(relax(diffs, laps, state[x], base, rate, mix))
        state = fresh
    for x in range(BXC):
        for c in range(4):
            done[pl.ds((c * BXC + x) * ROWS, ROWS), :] = state[x][c]
    for block in range(ROWS):
        out_ref[owner_ref[0, block]] = done[pl.ds(block, 4 * BXC, stride=ROWS), :]


def on_device(initial_field, base_reluctivity, saturation_rate, mixing, face_contact, new_owner):
    f32 = jnp.float32
    cells = BLY * BYC
    peers = lax.axis_size("seg")
    own, up, down = pl.pallas_call(
        pack_kernel,
        out_shape=(
            jax.ShapeDtypeStruct((HFC, LANES), f32),
            jax.ShapeDtypeStruct((SLABS + ROWS, LANES), f32),
            jax.ShapeDtypeStruct((SLABS + ROWS, LANES), f32),
        ),
        in_specs=[VMEM, VMEM, VMEM, SMEM],
        out_specs=(VMEM, VMEM, VMEM),
        compiler_params=pltpu.CompilerParams(vmem_limit_bytes=4 << 20),
        name="pack",
    )(
        initial_field.reshape(4 * BXC * cells, BLZ * BZC),
        base_reluctivity.reshape(BXC * cells, BLZ * BZC),
        saturation_rate.reshape(BXC * cells, BLZ * BZC),
        face_contact[0].T,
    )

    def both_ways(to_next, to_last, axis):
        size = lax.axis_size(axis)
        rising = [(i, i + 1) for i in range(size - 1)]
        falling = [(j, i) for i, j in rising]
        return lax.ppermute(to_next, axis, rising), lax.ppermute(to_last, axis, falling)

    below, above = both_ways(up, down, "seg")
    package = pl.pallas_call(
        join_kernel,
        out_shape=jax.ShapeDtypeStruct((PACK, LANES), f32),
        in_specs=[VMEM] * 3,
        out_specs=VMEM,
        compiler_params=pltpu.CompilerParams(vmem_limit_bytes=4 << 20),
        name="join",
    )(own, below, above)
    low, high = both_ways(package, package, "grp")
    placed = pl.pallas_call(
        update_kernel,
        out_shape=jax.ShapeDtypeStruct((peers, 4 * BXC, LANES), f32),
        in_specs=[SMEM, SMEM, VMEM, VMEM, VMEM],
        out_specs=VMEM,
        scratch_shapes=[
            pltpu.VMEM((2, EXT * CH * RING + 2 * PAD, LANES), f32),
            pltpu.VMEM((3, 3, 8, ROWS, LANES), f32),
            pltpu.VMEM((4 * BXC * ROWS, LANES), f32),
        ],
        compiler_params=pltpu.CompilerParams(vmem_limit_bytes=8 << 20),
        name="update",
    )(mixing, new_owner, package, low, high)
    received = lax.all_to_all(placed, "seg", split_axis=0, concat_axis=0, tiled=True)
    return received.reshape(peers, 4, BXC, LANES)


def solution(mesh):
    return jax.shard_map(
        on_device,
        mesh=mesh,
        in_specs=(
            P(None, "grp", "seg", None),
            P("grp", "seg", None),
            P("grp", "seg", None),
            P(),
            P("grp", "seg", None),
            P("grp", "seg"),
        ),
        out_specs=P(("grp", "seg"), None, None, None),
        check_vma=False,
    )
```

```python
import jax
import jax.numpy as jnp
from jax import lax
from jax.experimental import pallas as pl
from jax.experimental.pallas import tpu as pltpu
from jax.sharding import PartitionSpec as P

BXC = 4
BYC = 16
BZC = 8
BLY = 2
BLZ = 4
STEPS1 = 4
STEPS2 = 4
ROWS = BLY * BLZ
LANES = BYC * BZC
CH = 6
SLABS = CH * BXC
FC = SLABS * ROWS
OWN = FC + ROWS
EDGE = 3 * SLABS + 3 * ROWS
EXT = 3 * BXC
step_size = 0.05

VMEM = pl.BlockSpec(memory_space=pltpu.VMEM)
SMEM = pl.BlockSpec(memory_space=pltpu.SMEM)
HBM = pl.BlockSpec(memory_space=pltpu.HBM)


def iotas():
    row = lax.broadcasted_iota(jnp.int32, (ROWS, LANES), 0)
    lane = lax.broadcasted_iota(jnp.int32, (ROWS, LANES), 1)
    return row, lane


def lanes_of(rows):
    return lax.broadcasted_iota(jnp.int32, (rows, LANES), 1)


def lroll(value, shift):
    return value if shift % LANES == 0 else pltpu.roll(value, shift % LANES, 1)


def sroll(value, shift):
    return pltpu.roll(value, shift % ROWS, 0)


def pack_kernel(
    field_hbm, base_hbm, rate_hbm, contact_ref, own_ref, field_ref, base_ref, rate_ref, sems
):
    copies = [
        pltpu.make_async_copy(source, target, sems.at[n])
        for n, (source, target) in enumerate(
            ((field_hbm, field_ref), (base_hbm, base_ref), (rate_hbm, rate_ref))
        )
    ]
    for copy in copies:
        copy.start()
    row, lane = iotas()
    contact = jnp.zeros((ROWS, LANES), jnp.float32)
    for d in range(6):
        for block in range(ROWS):
            here = jnp.logical_and(row == block, lane == d)
            contact = jnp.where(here, contact_ref[d, 0, block].astype(jnp.float32), contact)
    own_ref[pl.ds(FC, ROWS), :] = contact
    for copy in copies:
        copy.wait()
    first = 0
    for ref, slabs in ((field_ref, 4 * BXC), (base_ref, BXC), (rate_ref, BXC)):
        count = slabs * BLY
        group = lanes_of(count) // BZC % BLZ
        placed = [None] * BLZ
        for q in range(BLZ):
            mixed = jnp.concatenate(
                [ref[pl.ds(BLZ * r + q, count, stride=BYC), :] for r in range(BLZ)], axis=1
            )
            for kz in range(BLZ):
                moved = lroll(mixed, BZC * (q - kz))
                placed[kz] = moved if q == 0 else jnp.where(group == q, moved, placed[kz])
        for kz in range(BLZ):
            own_ref[pl.ds(first * ROWS + kz, count, stride=BLZ), :] = placed[kz]
        first += slabs


def stage_kernel(own_ref, local_ref):
    local_ref[...] = own_ref[...]


def edge_kernel(own_ref, inside_ref, across_ref, second_ref, first_ref):
    even = lax.axis_index("seg") % 2 == 0
    quarter = lanes_of(SLABS) // (LANES // 4)
    for part, ref in enumerate((own_ref, inside_ref, across_ref)):
        edges = []
        for jy, start in ((BLY - 1, LANES - LANES // 4), (0, 0)):
            edge = None
            for kz in range(BLZ):
                value = ref[pl.ds(jy * BLZ + kz, SLABS, stride=ROWS), :]
                moved = lroll(value, kz * (LANES // 4) - start)
                edge = moved if kz == 0 else jnp.where(quarter == kz, moved, edge)
            edges.append(edge)
        up, down = edges
        contact = ref[pl.ds(FC, ROWS), :]
        first_ref[pl.ds(part * SLABS, SLABS), :] = jnp.where(even, up, down)
        second_ref[pl.ds(part * SLABS, SLABS), :] = jnp.where(even, down, up)
        for out_ref in (first_ref, second_ref):
            out_ref[pl.ds(3 * SLABS + part * ROWS, ROWS), :] = contact


def relax(differences, laplacian, values, base, rate, mix):
    e_xh, e_yh, e_zh = differences
    field_x = e_yh[2] - e_zh[1]
    field_y = e_zh[0] - e_xh[2]
    field_z = e_xh[1] - e_yh[0]
    saturation = rate * (field_x * field_x + field_y * field_y + field_z * field_z)
    reluctivity = base * (3.0 - 2.0 / (1.0 + saturation))
    updated = []
    for channel in range(4):
        total = reluctivity * laplacian[channel]
        for source in range(4):
            total = total + mix[channel][source] * values[source]
        updated.append(total)
    return updated


RING = 2 * ROWS
PAD = ROWS


def update_kernel(mix_hbm, owner_hbm, own_ref, inside_ref, across_ref, first_ref, second_ref, out_ref, *scratch):
    ring, cin, done, mix_ref, owner_ref, sems = scratch
    copies = [
        pltpu.make_async_copy(mix_hbm, mix_ref, sems.at[0]),
        pltpu.make_async_copy(owner_hbm, owner_ref, sems.at[1]),
    ]
    for copy in copies:
        copy.start()
    even_x = lax.axis_index("grp") % 2 == 0
    even_y = lax.axis_index("seg") % 2 == 0
    places = (1, jnp.where(even_x, 2, 0), jnp.where(even_x, 0, 2))
    row, lane = iotas()
    kz, yi, zi = row % BLZ, lane // BZC, lane % BZC
    first_half = row < BLZ
    one = jnp.ones((ROWS, LANES), jnp.float32)
    zero = jnp.zeros((ROWS, LANES), jnp.float32)
    total = EXT * CH * RING

    def at(i, channel):
        return PAD + (i // BXC * SLABS + channel * BXC + i % BXC) * RING

    for now in range(2):
        ring[now, pl.ds(0, PAD), :] = zero
        ring[now, pl.ds(PAD + total, PAD), :] = zero
    for i, channel in ((0, 1), (0, 2), (0, 3), (0, 4), (BXC, 4)):
        ring[1, pl.ds(at(i, channel), ROWS), :] = zero
    for i, channel in ((BXC - 1, 5), (2 * BXC - 1, 5), (EXT - 1, 0), (EXT - 1, 1), (EXT - 1, 2)):
        ring[1, pl.ds(at(i, channel) + ROWS, ROWS), :] = zero
    for n, ref in enumerate((own_ref, inside_ref, across_ref)):
        part = places[n]
        begin = PAD + part * SLABS * RING
        if n > 0:
            begin = pl.multiple_of(begin, ROWS)
        for slab in range(SLABS):
            ring[0, pl.ds(begin + slab * RING + BLZ, ROWS), :] = ref[pl.ds(slab * ROWS, ROWS), :]
        first = first_ref[pl.ds(n * SLABS, SLABS), :]
        second = second_ref[pl.ds(n * SLABS, SLABS), :]
        compact_low = jnp.where(even_y, second, first)
        compact_high = jnp.where(even_y, first, second)
        wide_lane = lanes_of(SLABS)
        for k in range(BLZ):
            below = lroll(compact_low, LANES - (k + 1) * (LANES // 4))
            above = lroll(compact_high, -k * (LANES // 4))
            beyond = jnp.where(wide_lane >= LANES - LANES // 4, below, 0.0)
            beyond = jnp.where(wide_lane < LANES // 4, above, beyond)
            ring[0, pl.ds(begin + k, SLABS, stride=RING), :] = beyond
            ring[0, pl.ds(begin + k + 3 * BLZ, SLABS, stride=RING), :] = beyond
        contact = ref[pl.ds(FC, ROWS), :]
        first = first_ref[pl.ds(3 * SLABS + n * ROWS, ROWS), :]
        second = second_ref[pl.ds(3 * SLABS + n * ROWS, ROWS), :]
        faces = []
        beside = sroll(jnp.where(first_half == even_y, first, second), BLZ)
        for d in range(6):
            ab = jnp.broadcast_to(contact[:, d : d + 1], (ROWS, LANES))
            ba = sroll(ab, BLZ)
            owners = jnp.broadcast_to(beside[:, d : d + 1], (ROWS, LANES))
            c = jnp.where(lane < LANES // 2, sroll(owners, BLZ), owners)
            ca = jnp.where(first_half, c, ba)
            bc = jnp.where(first_half, ba, sroll(c, BLZ))
            faces.append((ca, bc, ab))
        for g in range(3):
            f = [faces[d][g] for d in range(6)]
            ylow = jnp.where(yi == 0, f[2], one)
            yhigh = jnp.where(yi == BYC - 1, f[3], one)
            zlow = jnp.where(zi == 0, f[4], one)
            zlow_n = jnp.where(jnp.logical_and(zi == 0, kz == 0), 0.0, zlow)
            zhigh = jnp.where(zi == BZC - 1, f[5], one)
            zhigh_n = jnp.where(jnp.logical_and(zi == BZC - 1, kz == BLZ - 1), 0.0, zhigh)
            entries = (ylow, yhigh, zlow_n, zhigh, zhigh_n, ylow + zlow, f[0], f[1])
            for d, entry in enumerate(entries):
                cin[part, g, d] = entry

    def put(now, start, value):
        ring[now, pl.ds(start, ROWS), :] = value

    def sweep(now, i, last):
        part, x = i // BXC, i % BXC
        groups = (2,) if last else (0, 1)
        offset = {0: 0, 1: ROWS, 2: BLZ}
        coefs = {g: [cin[part, g, d] for d in range(8)] for g in groups}
        laps = {g: [] for g in groups}
        diffs = {g: ([], [], []) for g in groups}
        values = {g: [] for g in groups}
        for c in range(4):
            start, before, after = at(i, c), at(i - 1, c), at(i + 1, c)

            def tile(begin):
                return ring[now, pl.ds(begin, ROWS), :]

            rows = [tile(start + offset[g]) for g in range(3)]
            following, previous = {0: 2, 1: 0, 2: 1}, {0: 1, 1: 2, 2: 0}
            ups = [lroll(v, -BZC) for v in rows]
            downs = [lroll(v, BZC) for v in rows]
            for g in groups:
                v = rows[g]
                cyl, cyh, nzl, czh, nzh, low, cxl, cxh = coefs[g]
                n_yh = jnp.where(yi < BYC - 1, ups[g], ups[following[g]])
                n_yl = jnp.where(yi > 0, downs[g], downs[previous[g]])
                z_next = lroll(tile(start + offset[g] + 1), BZC - 1)
                z_last = lroll(tile(start + offset[g] - 1), 1 - BZC)
                n_zh = jnp.where(zi < BZC - 1, lroll(v, -1), z_next)
                n_zl = jnp.where(zi > 0, lroll(v, 1), z_last)
                e_xl = v - tile(before + offset[g])
                if x == 0:
                    e_xl = cxl * e_xl
                e_xh = tile(after + offset[g]) - v
                if x == BXC - 1:
                    e_xh = cxh * e_xh
                e_yh = cyh * (n_yh - v)
                e_zh = nzh * n_zh - czh * v
                lap = (cyl * n_yl + nzl * n_zl) - low * v
                laps[g].append((lap - e_xl) + (e_xh + (e_yh + e_zh)))
                diffs[g][0].append(e_xh)
                diffs[g][1].append(e_yh)
                diffs[g][2].append(e_zh)
                values[g].append(v)
        for g in groups:
            base = ring[0, pl.ds(at(i, 4) + offset[g], ROWS), :] * step_size
            rate = ring[0, pl.ds(at(i, 5) + offset[g], ROWS), :]
            updated = relax(diffs[g], laps[g], values[g], base, rate, mix)
            if last:
                state[x] = updated
            else:
                for c in range(4):
                    put(1 - now, at(i, c) + offset[g], updated[c])

    for copy in copies:
        copy.wait()
    mix = [
        [step_size * mix_ref[c, e] + (1.0 if c == e else 0.0) for e in range(4)] for c in range(4)
    ]
    state = [None] * BXC
    for step in range(STEPS1):
        for i in range(step + 1, EXT - 1 - step):
            sweep(step % 2, i, step == STEPS1 - 1)

    y_inner = jnp.where(yi < BYC - 1, 1.0, 0.0)
    z_inner = jnp.where(zi < BZC - 1, 1.0, 0.0)
    y_low_inner = jnp.where(yi > 0, 1.0, 0.0)
    z_low_inner = jnp.where(zi > 0, 1.0, 0.0)
    out_ref[...] = jnp.zeros_like(out_ref)
    for _ in range(STEPS2):
        fresh = []
        rise = [[state[x + 1][c] - state[x][c] for c in range(4)] for x in range(BXC - 1)]
        rise.append([zero] * 4)
        for x in range(BXC):
            laps, diffs = [], ([], [], [])
            for c in range(4):
                v = state[x][c]
                e_yh = y_inner * (lroll(v, -BZC) - v)
                e_zh = z_inner * (lroll(v, -1) - v)
                e_yl = y_low_inner * (lroll(v, BZC) - v)
                e_zl = z_low_inner * (lroll(v, 1) - v)
                lap = (e_yl + e_yh) + (e_zl + e_zh)
                if x < BXC - 1:
                    lap = lap + rise[x][c]
                if x > 0:
                    lap = lap - rise[x - 1][c]
                laps.append(lap)
                diffs[0].append(rise[x][c])
                diffs[1].append(e_yh)
                diffs[2].append(e_zh)
            base = ring[0, pl.ds(at(BXC + x, 4) + BLZ, ROWS), :] * step_size
            rate = ring[0, pl.ds(at(BXC + x, 5) + BLZ, ROWS), :]
            fresh.append(relax(diffs, laps, state[x], base, rate, mix))
        state = fresh
    for x in range(BXC):
        for c in range(4):
            done[pl.ds((c * BXC + x) * ROWS, ROWS), :] = state[x][c]
    for block in range(ROWS):
        out_ref[owner_ref[0, block]] = done[pl.ds(block, 4 * BXC, stride=ROWS), :]


def on_device(initial_field, base_reluctivity, saturation_rate, mixing, face_contact, new_owner):
    f32 = jnp.float32
    cells = BLY * BYC
    peers = lax.axis_size("seg")
    small = pltpu.CompilerParams(vmem_limit_bytes=4 << 20)
    own = pl.pallas_call(
        pack_kernel,
        out_shape=jax.ShapeDtypeStruct((OWN, LANES), f32),
        in_specs=[HBM, HBM, HBM, SMEM],
        out_specs=VMEM,
        scratch_shapes=[
            pltpu.VMEM((4 * BXC * cells, BLZ * BZC), f32),
            pltpu.VMEM((BXC * cells, BLZ * BZC), f32),
            pltpu.VMEM((BXC * cells, BLZ * BZC), f32),
            pltpu.SemaphoreType.DMA((3,)),
        ],
        compiler_params=pltpu.CompilerParams(vmem_limit_bytes=66_900_000),
        name="pack",
    )(
        initial_field.reshape(4 * BXC * cells, BLZ * BZC),
        base_reluctivity.reshape(BXC * cells, BLZ * BZC),
        saturation_rate.reshape(BXC * cells, BLZ * BZC),
        face_contact.transpose(2, 0, 1),
    )

    def swap(value, axis, offset):
        pairs = [(i, i + 1) for i in range(offset, lax.axis_size(axis) - 1, 2)]
        return lax.ppermute(value, axis, pairs + [(j, i) for i, j in pairs])

    inside = swap(own, "grp", 0)
    across = swap(own, "grp", 1)
    own = pl.pallas_call(
        stage_kernel,
        out_shape=jax.ShapeDtypeStruct((OWN, LANES), f32),
        in_specs=[VMEM],
        out_specs=VMEM,
        compiler_params=small,
        name="stage_own",
    )(own)
    second, first = pl.pallas_call(
        edge_kernel,
        out_shape=(
            jax.ShapeDtypeStruct((EDGE, LANES), f32),
            jax.ShapeDtypeStruct((EDGE, LANES), f32),
        ),
        in_specs=[VMEM] * 3,
        out_specs=(VMEM, VMEM),
        compiler_params=small,
        name="edge",
    )(own, inside, across)
    first = swap(first, "seg", 0)
    second = swap(second, "seg", 1)
    placed = pl.pallas_call(
        update_kernel,
        out_shape=jax.ShapeDtypeStruct((peers, 4 * BXC, LANES), f32),
        in_specs=[HBM, HBM] + [VMEM] * 5,
        out_specs=VMEM,
        scratch_shapes=[
            pltpu.VMEM((2, EXT * CH * RING + 2 * PAD, LANES), f32),
            pltpu.VMEM((3, 3, 8, ROWS, LANES), f32),
            pltpu.VMEM((4 * BXC * ROWS, LANES), f32),
            pltpu.SMEM((4, 4), f32),
            pltpu.SMEM((1, BLY * BLZ), jnp.int32),
            pltpu.SemaphoreType.DMA((2,)),
        ],
        compiler_params=pltpu.CompilerParams(vmem_limit_bytes=8 << 20),
        name="update",
    )(mixing, new_owner, own, inside, across, first, second)
    received = lax.all_to_all(
        placed.reshape(peers, 4, BXC, LANES), "seg", split_axis=0, concat_axis=0, tiled=True
    )
    return received


def solution(mesh):
    return jax.shard_map(
        on_device,
        mesh=mesh,
        in_specs=(
            P(None, "grp", "seg", None),
            P("grp", "seg", None),
            P("grp", "seg", None),
            P(),
            P("grp", "seg", None),
            P("grp", "seg"),
        ),
        out_specs=P(("grp", "seg"), None, None, None),
        check_vma=False,
    )
```

```python
import jax
import jax.numpy as jnp
from jax import lax
from jax.experimental import pallas as pl
from jax.experimental.pallas import tpu as pltpu
from jax.sharding import PartitionSpec as P

BXC = 4
BYC = 16
BZC = 8
BLY = 2
BLZ = 4
STEPS1 = 4
STEPS2 = 4
ROWS = BLY * BLZ
LANES = BYC * BZC
CH = 6
SLABS = CH * BXC
FC = SLABS * ROWS
OWN = FC + ROWS
EDGE = 3 * SLABS + 3 * ROWS
EXT = 3 * BXC
step_size = 0.05

VMEM = pl.BlockSpec(memory_space=pltpu.VMEM)
SMEM = pl.BlockSpec(memory_space=pltpu.SMEM)
HBM = pl.BlockSpec(memory_space=pltpu.HBM)


def in_hbm(value):
    return pltpu.with_memory_space_constraint(value, pltpu.HBM)


def iotas():
    row = lax.broadcasted_iota(jnp.int32, (ROWS, LANES), 0)
    lane = lax.broadcasted_iota(jnp.int32, (ROWS, LANES), 1)
    return row, lane


def lanes_of(rows):
    return lax.broadcasted_iota(jnp.int32, (rows, LANES), 1)


def lroll(value, shift):
    return value if shift % LANES == 0 else pltpu.roll(value, shift % LANES, 1)


def sroll(value, shift):
    return pltpu.roll(value, shift % ROWS, 0)


def pack_kernel(
    field_hbm,
    base_hbm,
    rate_hbm,
    contact_hbm,
    own_ref,
    field_ref,
    base_ref,
    rate_ref,
    contact_ref,
    sems,
):
    copies = [
        pltpu.make_async_copy(source, target, sems.at[n])
        for n, (source, target) in enumerate(
            (
                (contact_hbm, contact_ref),
                (base_hbm, base_ref),
                (rate_hbm, rate_ref),
                (field_hbm, field_ref),
            )
        )
    ]
    for copy in copies:
        copy.start()
    copies[0].wait()
    row, lane = iotas()
    contact = jnp.zeros((ROWS, LANES), jnp.float32)
    for d in range(6):
        for block in range(ROWS):
            here = jnp.logical_and(row == block, lane == d)
            contact = jnp.where(here, contact_ref[d, 0, block].astype(jnp.float32), contact)
    own_ref[pl.ds(FC, ROWS), :] = contact
    for copy in copies[1:]:
        copy.wait()
    first = 0
    for ref, slabs in ((field_ref, 4 * BXC), (base_ref, BXC), (rate_ref, BXC)):
        count = slabs * BLY
        group = lanes_of(count) // BZC % BLZ
        placed = [None] * BLZ
        for q in range(BLZ):
            mixed = jnp.concatenate(
                [ref[pl.ds(BLZ * r + q, count, stride=BYC), :] for r in range(BLZ)], axis=1
            )
            for kz in range(BLZ):
                moved = lroll(mixed, BZC * (q - kz))
                placed[kz] = moved if q == 0 else jnp.where(group == q, moved, placed[kz])
        for kz in range(BLZ):
            own_ref[pl.ds(first * ROWS + kz, count, stride=BLZ), :] = placed[kz]
        first += slabs


def edge_kernel(own_ref, inside_ref, across_ref, second_ref, first_ref):
    even = lax.axis_index("seg") % 2 == 0
    quarter = lanes_of(SLABS) // (LANES // 4)
    for part, ref in enumerate((own_ref, inside_ref, across_ref)):
        edges = []
        for jy, start in ((BLY - 1, LANES - LANES // 4), (0, 0)):
            edge = None
            for kz in range(BLZ):
                value = ref[pl.ds(jy * BLZ + kz, SLABS, stride=ROWS), :]
                moved = lroll(value, kz * (LANES // 4) - start)
                edge = moved if kz == 0 else jnp.where(quarter == kz, moved, edge)
            edges.append(edge)
        up, down = edges
        contact = ref[pl.ds(FC, ROWS), :]
        first_ref[pl.ds(part * SLABS, SLABS), :] = jnp.where(even, up, down)
        second_ref[pl.ds(part * SLABS, SLABS), :] = jnp.where(even, down, up)
        for out_ref in (first_ref, second_ref):
            out_ref[pl.ds(3 * SLABS + part * ROWS, ROWS), :] = contact


def relax(differences, laplacian, values, base, rate, mix):
    e_xh, e_yh, e_zh = differences
    field_x = e_yh[2] - e_zh[1]
    field_y = e_zh[0] - e_xh[2]
    field_z = e_xh[1] - e_yh[0]
    saturation = rate * (field_x * field_x + field_y * field_y + field_z * field_z)
    reluctivity = base * (3.0 - 2.0 / (1.0 + saturation))
    updated = []
    for channel in range(4):
        total = reluctivity * laplacian[channel]
        for source in range(4):
            total = total + mix[channel][source] * values[source]
        updated.append(total)
    return updated


RING = 2 * ROWS
PAD = ROWS


def update_kernel(mix_hbm, owner_hbm, own_ref, inside_ref, across_ref, first_ref, second_ref, out_ref, *scratch):
    ring, cin, done, mix_ref, owner_ref, sems = scratch
    copies = [
        pltpu.make_async_copy(mix_hbm, mix_ref, sems.at[0]),
        pltpu.make_async_copy(owner_hbm, owner_ref, sems.at[1]),
    ]
    for copy in copies:
        copy.start()
    even_x = lax.axis_index("grp") % 2 == 0
    even_y = lax.axis_index("seg") % 2 == 0
    places = (1, jnp.where(even_x, 2, 0), jnp.where(even_x, 0, 2))
    row, lane = iotas()
    kz, yi, zi = row % BLZ, lane // BZC, lane % BZC
    first_half = row < BLZ
    one = jnp.ones((ROWS, LANES), jnp.float32)
    zero = jnp.zeros((ROWS, LANES), jnp.float32)
    total = EXT * CH * RING

    def at(i, channel):
        return PAD + (i // BXC * SLABS + channel * BXC + i % BXC) * RING

    for now in range(2):
        ring[now, pl.ds(0, PAD), :] = zero
        ring[now, pl.ds(PAD + total, PAD), :] = zero
    for i, channel in ((0, 1), (0, 2), (0, 3), (0, 4), (BXC, 4)):
        ring[1, pl.ds(at(i, channel), ROWS), :] = zero
    for i, channel in ((BXC - 1, 5), (2 * BXC - 1, 5), (EXT - 1, 0), (EXT - 1, 1), (EXT - 1, 2)):
        ring[1, pl.ds(at(i, channel) + ROWS, ROWS), :] = zero
    for n, ref in enumerate((own_ref, inside_ref, across_ref)):
        part = places[n]
        begin = PAD + part * SLABS * RING
        if n > 0:
            begin = pl.multiple_of(begin, ROWS)
        for slab in range(SLABS):
            ring[0, pl.ds(begin + slab * RING + BLZ, ROWS), :] = ref[pl.ds(slab * ROWS, ROWS), :]
        first = first_ref[pl.ds(n * SLABS, SLABS), :]
        second = second_ref[pl.ds(n * SLABS, SLABS), :]
        compact_low = jnp.where(even_y, second, first)
        compact_high = jnp.where(even_y, first, second)
        wide_lane = lanes_of(SLABS)
        for k in range(BLZ):
            below = lroll(compact_low, LANES - (k + 1) * (LANES // 4))
            above = lroll(compact_high, -k * (LANES // 4))
            beyond = jnp.where(wide_lane >= LANES - LANES // 4, below, 0.0)
            beyond = jnp.where(wide_lane < LANES // 4, above, beyond)
            ring[0, pl.ds(begin + k, SLABS, stride=RING), :] = beyond
            ring[0, pl.ds(begin + k + 3 * BLZ, SLABS, stride=RING), :] = beyond
        contact = ref[pl.ds(FC, ROWS), :]
        first = first_ref[pl.ds(3 * SLABS + n * ROWS, ROWS), :]
        second = second_ref[pl.ds(3 * SLABS + n * ROWS, ROWS), :]
        faces = []
        beside = sroll(jnp.where(first_half == even_y, first, second), BLZ)
        for d in range(6):
            ab = jnp.broadcast_to(contact[:, d : d + 1], (ROWS, LANES))
            ba = sroll(ab, BLZ)
            owners = jnp.broadcast_to(beside[:, d : d + 1], (ROWS, LANES))
            c = jnp.where(lane < LANES // 2, sroll(owners, BLZ), owners)
            ca = jnp.where(first_half, c, ba)
            bc = jnp.where(first_half, ba, sroll(c, BLZ))
            faces.append((ca, bc, ab))
        for g in range(3):
            f = [faces[d][g] for d in range(6)]
            ylow = jnp.where(yi == 0, f[2], one)
            yhigh = jnp.where(yi == BYC - 1, f[3], one)
            zlow = jnp.where(zi == 0, f[4], one)
            zlow_n = jnp.where(jnp.logical_and(zi == 0, kz == 0), 0.0, zlow)
            zhigh = jnp.where(zi == BZC - 1, f[5], one)
            zhigh_n = jnp.where(jnp.logical_and(zi == BZC - 1, kz == BLZ - 1), 0.0, zhigh)
            entries = (ylow, yhigh, zlow_n, zhigh, zhigh_n, ylow + zlow, f[0], f[1])
            for d, entry in enumerate(entries):
                cin[part, g, d] = entry

    def put(now, start, value):
        ring[now, pl.ds(start, ROWS), :] = value

    def sweep(now, i, last):
        part, x = i // BXC, i % BXC
        groups = (2,) if last else (0, 1)
        offset = {0: 0, 1: ROWS, 2: BLZ}
        coefs = {g: [cin[part, g, d] for d in range(8)] for g in groups}
        laps = {g: [] for g in groups}
        diffs = {g: ([], [], []) for g in groups}
        values = {g: [] for g in groups}
        for c in range(4):
            start, before, after = at(i, c), at(i - 1, c), at(i + 1, c)

            def tile(begin):
                return ring[now, pl.ds(begin, ROWS), :]

            rows = [tile(start + offset[g]) for g in range(3)]
            following, previous = {0: 2, 1: 0, 2: 1}, {0: 1, 1: 2, 2: 0}
            ups = [lroll(v, -BZC) for v in rows]
            downs = [lroll(v, BZC) for v in rows]
            for g in groups:
                v = rows[g]
                cyl, cyh, nzl, czh, nzh, low, cxl, cxh = coefs[g]
                n_yh = jnp.where(yi < BYC - 1, ups[g], ups[following[g]])
                n_yl = jnp.where(yi > 0, downs[g], downs[previous[g]])
                z_next = lroll(tile(start + offset[g] + 1), BZC - 1)
                z_last = lroll(tile(start + offset[g] - 1), 1 - BZC)
                n_zh = jnp.where(zi < BZC - 1, lroll(v, -1), z_next)
                n_zl = jnp.where(zi > 0, lroll(v, 1), z_last)
                e_xl = v - tile(before + offset[g])
                if x == 0:
                    e_xl = cxl * e_xl
                e_xh = tile(after + offset[g]) - v
                if x == BXC - 1:
                    e_xh = cxh * e_xh
                e_yh = cyh * (n_yh - v)
                e_zh = nzh * n_zh - czh * v
                lap = (cyl * n_yl + nzl * n_zl) - low * v
                laps[g].append((lap - e_xl) + (e_xh + (e_yh + e_zh)))
                diffs[g][0].append(e_xh)
                diffs[g][1].append(e_yh)
                diffs[g][2].append(e_zh)
                values[g].append(v)
        for g in groups:
            base = ring[0, pl.ds(at(i, 4) + offset[g], ROWS), :] * step_size
            rate = ring[0, pl.ds(at(i, 5) + offset[g], ROWS), :]
            updated = relax(diffs[g], laps[g], values[g], base, rate, mix)
            if last:
                state[x] = updated
            else:
                for c in range(4):
                    put(1 - now, at(i, c) + offset[g], updated[c])

    for copy in copies:
        copy.wait()
    mix = [
        [step_size * mix_ref[c, e] + (1.0 if c == e else 0.0) for e in range(4)] for c in range(4)
    ]
    state = [None] * BXC
    for step in range(STEPS1):
        for i in range(step + 1, EXT - 1 - step):
            sweep(step % 2, i, step == STEPS1 - 1)

    y_inner = jnp.where(yi < BYC - 1, 1.0, 0.0)
    z_inner = jnp.where(zi < BZC - 1, 1.0, 0.0)
    y_low_inner = jnp.where(yi > 0, 1.0, 0.0)
    z_low_inner = jnp.where(zi > 0, 1.0, 0.0)
    out_ref[...] = jnp.zeros_like(out_ref)
    for _ in range(STEPS2):
        fresh = []
        rise = [[state[x + 1][c] - state[x][c] for c in range(4)] for x in range(BXC - 1)]
        rise.append([zero] * 4)
        for x in range(BXC):
            laps, diffs = [], ([], [], [])
            for c in range(4):
                v = state[x][c]
                e_yh = y_inner * (lroll(v, -BZC) - v)
                e_zh = z_inner * (lroll(v, -1) - v)
                e_yl = y_low_inner * (lroll(v, BZC) - v)
                e_zl = z_low_inner * (lroll(v, 1) - v)
                lap = (e_yl + e_yh) + (e_zl + e_zh)
                if x < BXC - 1:
                    lap = lap + rise[x][c]
                if x > 0:
                    lap = lap - rise[x - 1][c]
                laps.append(lap)
                diffs[0].append(rise[x][c])
                diffs[1].append(e_yh)
                diffs[2].append(e_zh)
            base = ring[0, pl.ds(at(BXC + x, 4) + BLZ, ROWS), :] * step_size
            rate = ring[0, pl.ds(at(BXC + x, 5) + BLZ, ROWS), :]
            fresh.append(relax(diffs, laps, state[x], base, rate, mix))
        state = fresh
    for x in range(BXC):
        for c in range(4):
            done[pl.ds((c * BXC + x) * ROWS, ROWS), :] = state[x][c]
    for block in range(ROWS):
        out_ref[owner_ref[0, block]] = done[pl.ds(block, 4 * BXC, stride=ROWS), :]


def on_device(initial_field, base_reluctivity, saturation_rate, mixing, face_contact, new_owner):
    f32 = jnp.float32
    cells = BLY * BYC
    peers = lax.axis_size("seg")
    small = pltpu.CompilerParams(vmem_limit_bytes=4 << 20)
    own = pl.pallas_call(
        pack_kernel,
        out_shape=jax.ShapeDtypeStruct((OWN, LANES), f32),
        in_specs=[HBM] * 4,
        out_specs=VMEM,
        scratch_shapes=[
            pltpu.VMEM((4 * BXC * cells, BLZ * BZC), f32),
            pltpu.VMEM((BXC * cells, BLZ * BZC), f32),
            pltpu.VMEM((BXC * cells, BLZ * BZC), f32),
            pltpu.SMEM((6, 1, ROWS), jnp.int32),
            pltpu.SemaphoreType.DMA((4,)),
        ],
        compiler_params=small,
        name="pack",
    )(
        in_hbm(initial_field.reshape(4 * BXC * cells, BLZ * BZC)),
        in_hbm(base_reluctivity.reshape(BXC * cells, BLZ * BZC)),
        in_hbm(saturation_rate.reshape(BXC * cells, BLZ * BZC)),
        in_hbm(face_contact.transpose(2, 0, 1)),
    )

    def swap(value, axis, offset):
        pairs = [(i, i + 1) for i in range(offset, lax.axis_size(axis) - 1, 2)]
        return lax.ppermute(value, axis, pairs + [(j, i) for i, j in pairs])

    inside = swap(own, "grp", 0)
    across = swap(own, "grp", 1)
    second, first = pl.pallas_call(
        edge_kernel,
        out_shape=(
            jax.ShapeDtypeStruct((EDGE, LANES), f32),
            jax.ShapeDtypeStruct((EDGE, LANES), f32),
        ),
        in_specs=[VMEM] * 3,
        out_specs=(VMEM, VMEM),
        compiler_params=small,
        name="edge",
    )(own, inside, across)
    first = swap(first, "seg", 0)
    second = swap(second, "seg", 1)
    placed = pl.pallas_call(
        update_kernel,
        out_shape=jax.ShapeDtypeStruct((peers, 4 * BXC, LANES), f32),
        in_specs=[HBM, HBM] + [VMEM] * 5,
        out_specs=VMEM,
        scratch_shapes=[
            pltpu.VMEM((2, EXT * CH * RING + 2 * PAD, LANES), f32),
            pltpu.VMEM((3, 3, 8, ROWS, LANES), f32),
            pltpu.VMEM((4 * BXC * ROWS, LANES), f32),
            pltpu.SMEM((4, 4), f32),
            pltpu.SMEM((1, BLY * BLZ), jnp.int32),
            pltpu.SemaphoreType.DMA((2,)),
        ],
        compiler_params=pltpu.CompilerParams(vmem_limit_bytes=8 << 20),
        name="update",
    )(in_hbm(mixing), in_hbm(new_owner), own, inside, across, first, second)
    received = lax.all_to_all(
        placed.reshape(peers, 4, BXC, LANES), "seg", split_axis=0, concat_axis=0, tiled=True
    )
    return received


def solution(mesh):
    return jax.shard_map(
        on_device,
        mesh=mesh,
        in_specs=(
            P(None, "grp", "seg", None),
            P("grp", "seg", None),
            P("grp", "seg", None),
            P(),
            P("grp", "seg", None),
            P("grp", "seg"),
        ),
        out_specs=P(("grp", "seg"), None, None, None),
        check_vma=False,
    )
```

```python
import jax
import jax.numpy as jnp
from jax import lax
from jax.experimental import pallas as pl
from jax.experimental.pallas import tpu as pltpu
from jax.sharding import PartitionSpec as P

BXC = 4
BYC = 16
BZC = 8
BLY = 2
BLZ = 4
STEPS1 = 4
STEPS2 = 4
ROWS = BLY * BLZ
LANES = BYC * BZC
CH = 6
SLABS = CH * BXC
FC = SLABS * ROWS
OWN = FC + ROWS
EDGE = 3 * SLABS + ROWS
EXT = 3 * BXC
step_size = 0.05

VMEM = pl.BlockSpec(memory_space=pltpu.VMEM)
SMEM = pl.BlockSpec(memory_space=pltpu.SMEM)
HBM = pl.BlockSpec(memory_space=pltpu.HBM)


def in_hbm(value):
    return pltpu.with_memory_space_constraint(value, pltpu.HBM)


def iotas():
    row = lax.broadcasted_iota(jnp.int32, (ROWS, LANES), 0)
    lane = lax.broadcasted_iota(jnp.int32, (ROWS, LANES), 1)
    return row, lane


def lanes_of(rows):
    return lax.broadcasted_iota(jnp.int32, (rows, LANES), 1)


def lroll(value, shift):
    return value if shift % LANES == 0 else pltpu.roll(value, shift % LANES, 1)


def sroll(value, shift):
    return pltpu.roll(value, shift % ROWS, 0)


def pack_kernel(
    field_hbm,
    base_hbm,
    rate_hbm,
    contact_hbm,
    own_ref,
    field_ref,
    base_ref,
    rate_ref,
    contact_ref,
    sems,
):
    cells = BXC * BLY * BYC
    parts = [(base_hbm, base_ref, 4), (rate_hbm, rate_ref, 5)]
    for c in range(4):
        parts.append((field_hbm.at[pl.ds(c * cells, cells)], field_ref.at[pl.ds(c * cells, cells)], c))
    contact_copy = pltpu.make_async_copy(contact_hbm, contact_ref, sems.at[6])
    contact_copy.start()
    copies = [
        pltpu.make_async_copy(source, target, sems.at[n])
        for n, (source, target, _) in enumerate(parts)
    ]
    for copy in copies:
        copy.start()
    contact_copy.wait()
    row, lane = iotas()
    contact = jnp.zeros((ROWS, LANES), jnp.float32)
    for d in range(6):
        for block in range(ROWS):
            here = jnp.logical_and(row == block, lane == d)
            contact = jnp.where(here, contact_ref[d, 0, block].astype(jnp.float32), contact)
    own_ref[pl.ds(FC, ROWS), :] = contact
    count = BXC * BLY
    for copy, (_, ref, channel) in zip(copies, parts):
        copy.wait()
        first = channel * BXC
        group = lanes_of(count) // BZC % BLZ
        placed = [None] * BLZ
        for q in range(BLZ):
            mixed = jnp.concatenate(
                [ref[pl.ds(BLZ * r + q, count, stride=BYC), :] for r in range(BLZ)], axis=1
            )
            for kz in range(BLZ):
                moved = lroll(mixed, BZC * (q - kz))
                placed[kz] = moved if q == 0 else jnp.where(group == q, moved, placed[kz])
        for kz in range(BLZ):
            own_ref[pl.ds(first * ROWS + kz, count, stride=BLZ), :] = placed[kz]


def edge_kernel(own_ref, inside_ref, across_ref, second_ref, first_ref):
    even = lax.axis_index("seg") % 2 == 0
    quarter = lanes_of(SLABS) // (LANES // 4)
    contact = None
    for part, ref in enumerate((own_ref, inside_ref, across_ref)):
        edges = []
        for jy, start in ((BLY - 1, LANES - LANES // 4), (0, 0)):
            edge = None
            for kz in range(BLZ):
                value = ref[pl.ds(jy * BLZ + kz, SLABS, stride=ROWS), :]
                moved = lroll(value, kz * (LANES // 4) - start)
                edge = moved if kz == 0 else jnp.where(quarter == kz, moved, edge)
            edges.append(edge)
        up, down = edges
        faces = lroll(ref[pl.ds(FC, ROWS), :], part * ROWS)
        contact = faces if part == 0 else contact + faces
        first_ref[pl.ds(part * SLABS, SLABS), :] = jnp.where(even, up, down)
        second_ref[pl.ds(part * SLABS, SLABS), :] = jnp.where(even, down, up)
    for out_ref in (first_ref, second_ref):
        out_ref[pl.ds(3 * SLABS, ROWS), :] = contact


def relax(differences, laplacian, values, base, rate, mix):
    e_xh, e_yh, e_zh = differences
    field_x = e_yh[2] - e_zh[1]
    field_y = e_zh[0] - e_xh[2]
    field_z = e_xh[1] - e_yh[0]
    saturation = rate * (field_x * field_x + field_y * field_y + field_z * field_z)
    reluctivity = base * (3.0 - 2.0 / (1.0 + saturation))
    updated = []
    for channel in range(4):
        total = reluctivity * laplacian[channel]
        for source in range(4):
            total = total + mix[channel][source] * values[source]
        updated.append(total)
    return updated


RING = 2 * ROWS
PAD = ROWS


def update_kernel(mix_hbm, owner_hbm, own_ref, inside_ref, across_ref, first_ref, second_ref, out_ref, *scratch):
    ring, cin, done, mix_ref, owner_ref, sems = scratch
    copies = [
        pltpu.make_async_copy(mix_hbm, mix_ref, sems.at[0]),
        pltpu.make_async_copy(owner_hbm, owner_ref, sems.at[1]),
    ]
    for copy in copies:
        copy.start()
    even_x = lax.axis_index("grp") % 2 == 0
    even_y = lax.axis_index("seg") % 2 == 0
    places = (1, jnp.where(even_x, 2, 0), jnp.where(even_x, 0, 2))
    row, lane = iotas()
    kz, yi, zi = row % BLZ, lane // BZC, lane % BZC
    first_half = row < BLZ
    up_lane = jnp.where(zi < BZC - 1, lane + 1, lane + 1 - BZC)
    down_lane = jnp.where(zi > 0, lane - 1, lane + BZC - 1)
    one = jnp.ones((ROWS, LANES), jnp.float32)
    zero = jnp.zeros((ROWS, LANES), jnp.float32)
    total = EXT * CH * RING

    def at(i, channel):
        return PAD + (i // BXC * SLABS + channel * BXC + i % BXC) * RING

    for now in range(2):
        ring[now, pl.ds(0, PAD), :] = zero
        ring[now, pl.ds(PAD + total, PAD), :] = zero
    for i, channel in ((0, 1), (0, 2), (0, 3), (0, 4), (BXC, 4)):
        ring[1, pl.ds(at(i, channel), ROWS), :] = zero
    for i, channel in ((BXC - 1, 5), (2 * BXC - 1, 5), (EXT - 1, 0), (EXT - 1, 1), (EXT - 1, 2)):
        ring[1, pl.ds(at(i, channel) + ROWS, ROWS), :] = zero
    for n, ref in enumerate((own_ref, inside_ref, across_ref)):
        part = places[n]
        begin = PAD + part * SLABS * RING
        if n > 0:
            begin = pl.multiple_of(begin, ROWS)
        for slab in range(SLABS):
            ring[0, pl.ds(begin + slab * RING + BLZ, ROWS), :] = ref[pl.ds(slab * ROWS, ROWS), :]
        first = first_ref[pl.ds(n * SLABS, SLABS), :]
        second = second_ref[pl.ds(n * SLABS, SLABS), :]
        compact_low = jnp.where(even_y, second, first)
        compact_high = jnp.where(even_y, first, second)
        wide_lane = lanes_of(SLABS)
        for k in range(BLZ):
            below = lroll(compact_low, LANES - (k + 1) * (LANES // 4))
            above = lroll(compact_high, -k * (LANES // 4))
            beyond = jnp.where(wide_lane >= LANES - LANES // 4, below, 0.0)
            beyond = jnp.where(wide_lane < LANES // 4, above, beyond)
            ring[0, pl.ds(begin + k, SLABS, stride=RING), :] = beyond
            ring[0, pl.ds(begin + k + 3 * BLZ, SLABS, stride=RING), :] = beyond
        contact = ref[pl.ds(FC, ROWS), :]
        first = first_ref[pl.ds(3 * SLABS, ROWS), :]
        second = second_ref[pl.ds(3 * SLABS, ROWS), :]
        faces = []
        beside = sroll(jnp.where(first_half == even_y, first, second), BLZ)
        for d in range(6):
            ab = jnp.broadcast_to(contact[:, d : d + 1], (ROWS, LANES))
            ba = sroll(ab, BLZ)
            at_lane = n * ROWS + d
            owners = jnp.broadcast_to(beside[:, at_lane : at_lane + 1], (ROWS, LANES))
            c = jnp.where(lane < LANES // 2, sroll(owners, BLZ), owners)
            ca = jnp.where(first_half, c, ba)
            bc = jnp.where(first_half, ba, sroll(c, BLZ))
            faces.append((ca, bc, ab))
        for g in range(3):
            f = [faces[d][g] for d in range(6)]
            ylow = jnp.where(yi == 0, f[2], one)
            yhigh = jnp.where(yi == BYC - 1, f[3], one)
            zlow = jnp.where(zi == 0, f[4], one)
            zlow_n = jnp.where(jnp.logical_and(zi == 0, kz == 0), 0.0, zlow)
            zhigh = jnp.where(zi == BZC - 1, f[5], one)
            zhigh_n = jnp.where(jnp.logical_and(zi == BZC - 1, kz == BLZ - 1), 0.0, zhigh)
            entries = (ylow, yhigh, zlow_n, zhigh, zhigh_n, ylow + zlow, f[0], f[1])
            for d, entry in enumerate(entries):
                cin[part, g, d] = entry

    def put(now, start, value):
        ring[now, pl.ds(start, ROWS), :] = value

    def sweep(now, i, last):
        part, x = i // BXC, i % BXC
        groups = (2,) if last else (0, 1)
        offset = {0: 0, 1: ROWS, 2: BLZ}
        coefs = {g: [cin[part, g, d] for d in range(8)] for g in groups}
        laps = {g: [] for g in groups}
        diffs = {g: ([], [], []) for g in groups}
        values = {g: [] for g in groups}
        for c in range(4):
            start, before, after = at(i, c), at(i - 1, c), at(i + 1, c)

            def tile(begin):
                return ring[now, pl.ds(begin, ROWS), :]

            rows = [tile(start + offset[g]) for g in range(3)]
            following, previous = {0: 2, 1: 0, 2: 1}, {0: 1, 1: 2, 2: 0}
            for g in groups:
                v = rows[g]
                cyl, cyh, nzl, czh, nzh, low, cxl, cxh = coefs[g]
                n_yh = lroll(jnp.where(yi == 0, rows[following[g]], v), -BZC)
                n_yl = lroll(jnp.where(yi == BYC - 1, rows[previous[g]], v), BZC)
                z_next = jnp.where(zi == 0, tile(start + offset[g] + 1), v)
                z_last = jnp.where(zi == BZC - 1, tile(start + offset[g] - 1), v)
                n_zh = jnp.take_along_axis(z_next, up_lane, axis=1)
                n_zl = jnp.take_along_axis(z_last, down_lane, axis=1)
                e_xl = v - tile(before + offset[g])
                if x == 0:
                    e_xl = cxl * e_xl
                e_xh = tile(after + offset[g]) - v
                if x == BXC - 1:
                    e_xh = cxh * e_xh
                e_yh = cyh * (n_yh - v)
                e_zh = nzh * n_zh - czh * v
                lap = (cyl * n_yl + nzl * n_zl) - low * v
                laps[g].append((lap - e_xl) + (e_xh + (e_yh + e_zh)))
                diffs[g][0].append(e_xh)
                diffs[g][1].append(e_yh)
                diffs[g][2].append(e_zh)
                values[g].append(v)
        for g in groups:
            base = ring[0, pl.ds(at(i, 4) + offset[g], ROWS), :] * step_size
            rate = ring[0, pl.ds(at(i, 5) + offset[g], ROWS), :]
            updated = relax(diffs[g], laps[g], values[g], base, rate, mix)
            if last:
                state[x] = updated
            else:
                for c in range(4):
                    put(1 - now, at(i, c) + offset[g], updated[c])

    for copy in copies:
        copy.wait()
    mix = [
        [step_size * mix_ref[c, e] + (1.0 if c == e else 0.0) for e in range(4)] for c in range(4)
    ]
    state = [None] * BXC
    for step in range(STEPS1):
        for i in range(step + 1, EXT - 1 - step):
            sweep(step % 2, i, step == STEPS1 - 1)

    y_inner = jnp.where(yi < BYC - 1, 1.0, 0.0)
    z_inner = jnp.where(zi < BZC - 1, 1.0, 0.0)
    y_low_inner = jnp.where(yi > 0, 1.0, 0.0)
    z_low_inner = jnp.where(zi > 0, 1.0, 0.0)
    out_ref[...] = jnp.zeros_like(out_ref)
    for _ in range(STEPS2):
        fresh = []
        rise = [[state[x + 1][c] - state[x][c] for c in range(4)] for x in range(BXC - 1)]
        rise.append([zero] * 4)
        for x in range(BXC):
            laps, diffs = [], ([], [], [])
            for c in range(4):
                v = state[x][c]
                e_yh = y_inner * (lroll(v, -BZC) - v)
                e_zh = z_inner * (lroll(v, -1) - v)
                e_yl = y_low_inner * (lroll(v, BZC) - v)
                e_zl = z_low_inner * (lroll(v, 1) - v)
                lap = (e_yl + e_yh) + (e_zl + e_zh)
                if x < BXC - 1:
                    lap = lap + rise[x][c]
                if x > 0:
                    lap = lap - rise[x - 1][c]
                laps.append(lap)
                diffs[0].append(rise[x][c])
                diffs[1].append(e_yh)
                diffs[2].append(e_zh)
            base = ring[0, pl.ds(at(BXC + x, 4) + BLZ, ROWS), :] * step_size
            rate = ring[0, pl.ds(at(BXC + x, 5) + BLZ, ROWS), :]
            fresh.append(relax(diffs, laps, state[x], base, rate, mix))
        state = fresh
    for x in range(BXC):
        for c in range(4):
            done[pl.ds((c * BXC + x) * ROWS, ROWS), :] = state[x][c]
    for block in range(ROWS):
        out_ref[owner_ref[0, block]] = done[pl.ds(block, 4 * BXC, stride=ROWS), :]


def on_device(initial_field, base_reluctivity, saturation_rate, mixing, face_contact, new_owner):
    f32 = jnp.float32
    cells = BLY * BYC
    peers = lax.axis_size("seg")
    small = pltpu.CompilerParams(vmem_limit_bytes=4 << 20)
    own = pl.pallas_call(
        pack_kernel,
        out_shape=jax.ShapeDtypeStruct((OWN, LANES), f32),
        in_specs=[HBM] * 4,
        out_specs=VMEM,
        scratch_shapes=[
            pltpu.VMEM((4 * BXC * cells, BLZ * BZC), f32),
            pltpu.VMEM((BXC * cells, BLZ * BZC), f32),
            pltpu.VMEM((BXC * cells, BLZ * BZC), f32),
            pltpu.SMEM((6, 1, ROWS), jnp.int32),
            pltpu.SemaphoreType.DMA((7,)),
        ],
        compiler_params=small,
        name="pack",
    )(
        in_hbm(initial_field.reshape(4 * BXC * cells, BLZ * BZC)),
        in_hbm(base_reluctivity.reshape(BXC * cells, BLZ * BZC)),
        in_hbm(saturation_rate.reshape(BXC * cells, BLZ * BZC)),
        in_hbm(face_contact.transpose(2, 0, 1)),
    )

    def swap(value, axis, offset):
        pairs = [(i, i + 1) for i in range(offset, lax.axis_size(axis) - 1, 2)]
        return lax.ppermute(value, axis, pairs + [(j, i) for i, j in pairs])

    inside = swap(own, "grp", 0)
    across = swap(own, "grp", 1)
    second, first = pl.pallas_call(
        edge_kernel,
        out_shape=(
            jax.ShapeDtypeStruct((EDGE, LANES), f32),
            jax.ShapeDtypeStruct((EDGE, LANES), f32),
        ),
        in_specs=[VMEM] * 3,
        out_specs=(VMEM, VMEM),
        compiler_params=small,
        name="edge",
    )(own, inside, across)
    first = swap(first, "seg", 0)
    second = swap(second, "seg", 1)
    placed = pl.pallas_call(
        update_kernel,
        out_shape=jax.ShapeDtypeStruct((peers, 4 * BXC, LANES), f32),
        in_specs=[HBM, HBM] + [VMEM] * 5,
        out_specs=VMEM,
        scratch_shapes=[
            pltpu.VMEM((2, EXT * CH * RING + 2 * PAD, LANES), f32),
            pltpu.VMEM((3, 3, 8, ROWS, LANES), f32),
            pltpu.VMEM((4 * BXC * ROWS, LANES), f32),
            pltpu.SMEM((4, 4), f32),
            pltpu.SMEM((1, BLY * BLZ), jnp.int32),
            pltpu.SemaphoreType.DMA((2,)),
        ],
        compiler_params=pltpu.CompilerParams(vmem_limit_bytes=8 << 20),
        name="update",
    )(in_hbm(mixing), in_hbm(new_owner), own, inside, across, first, second)
    received = lax.all_to_all(
        placed.reshape(peers, 4, BXC, LANES), "seg", split_axis=0, concat_axis=0, tiled=True
    )
    return received


def solution(mesh):
    return jax.shard_map(
        on_device,
        mesh=mesh,
        in_specs=(
            P(None, "grp", "seg", None),
            P("grp", "seg", None),
            P("grp", "seg", None),
            P(),
            P("grp", "seg", None),
            P("grp", "seg"),
        ),
        out_specs=P(("grp", "seg"), None, None, None),
        check_vma=False,
    )
```

```python
import jax
import jax.numpy as jnp
from jax import lax
from jax.experimental import pallas as pl
from jax.experimental.pallas import tpu as pltpu
from jax.sharding import PartitionSpec as P

BXC = 4
BYC = 16
BZC = 8
BLY = 2
BLZ = 4
STEPS1 = 4
STEPS2 = 4
ROWS = BLY * BLZ
LANES = BYC * BZC
CH = 6
SLABS = CH * BXC
FC = SLABS * ROWS
OWN = FC + ROWS
EDGE = 3 * SLABS + ROWS
EXT = 3 * BXC
step_size = 0.05

VMEM = pl.BlockSpec(memory_space=pltpu.VMEM)
SMEM = pl.BlockSpec(memory_space=pltpu.SMEM)
ANY = pl.BlockSpec(memory_space=pl.ANY)
HBM = pl.BlockSpec(memory_space=pltpu.HBM)


def in_hbm(value):
    return pltpu.with_memory_space_constraint(value, pltpu.HBM)


def iotas():
    row = lax.broadcasted_iota(jnp.int32, (ROWS, LANES), 0)
    lane = lax.broadcasted_iota(jnp.int32, (ROWS, LANES), 1)
    return row, lane


def lanes_of(rows):
    return lax.broadcasted_iota(jnp.int32, (rows, LANES), 1)


def lroll(value, shift):
    return value if shift % LANES == 0 else pltpu.roll(value, shift % LANES, 1)


def sroll(value, shift):
    return pltpu.roll(value, shift % ROWS, 0)


def pack_kernel(
    field_hbm,
    base_hbm,
    rate_hbm,
    contact_hbm,
    own_ref,
    field_ref,
    base_ref,
    rate_ref,
    contact_ref,
    sems,
):
    copies = [
        pltpu.make_async_copy(source, target, sems.at[n])
        for n, (source, target) in enumerate(
            (
                (contact_hbm, contact_ref),
                (base_hbm, base_ref),
                (rate_hbm, rate_ref),
                (field_hbm, field_ref),
            )
        )
    ]
    for copy in copies:
        copy.start()
    copies[0].wait()
    row, lane = iotas()
    contact = jnp.zeros((ROWS, LANES), jnp.float32)
    for d in range(6):
        for block in range(ROWS):
            here = jnp.logical_and(row == block, lane == d)
            contact = jnp.where(here, contact_ref[d, 0, block].astype(jnp.float32), contact)
    own_ref[pl.ds(FC, ROWS), :] = contact
    for copy in copies[1:]:
        copy.wait()
    first = 0
    for ref, slabs in ((field_ref, 4 * BXC), (base_ref, BXC), (rate_ref, BXC)):
        count = slabs * BLY
        group = lanes_of(count) // BZC % BLZ
        placed = [None] * BLZ
        for q in range(BLZ):
            mixed = jnp.concatenate(
                [ref[pl.ds(BLZ * r + q, count, stride=BYC), :] for r in range(BLZ)], axis=1
            )
            for kz in range(BLZ):
                moved = lroll(mixed, BZC * (q - kz))
                placed[kz] = moved if q == 0 else jnp.where(group == q, moved, placed[kz])
        for kz in range(BLZ):
            own_ref[pl.ds(first * ROWS + kz, count, stride=BLZ), :] = placed[kz]
        first += slabs


def edge_kernel(own_ref, inside_ref, across_ref, second_ref, first_ref):
    even = lax.axis_index("seg") % 2 == 0
    quarter = lanes_of(SLABS) // (LANES // 4)
    contact = None
    for part, ref in enumerate((own_ref, inside_ref, across_ref)):
        edges = []
        for jy, start in ((BLY - 1, LANES - LANES // 4), (0, 0)):
            edge = None
            for kz in range(BLZ):
                value = ref[pl.ds(jy * BLZ + kz, SLABS, stride=ROWS), :]
                moved = lroll(value, kz * (LANES // 4) - start)
                edge = moved if kz == 0 else jnp.where(quarter == kz, moved, edge)
            edges.append(edge)
        up, down = edges
        faces = lroll(ref[pl.ds(FC, ROWS), :], part * ROWS)
        contact = faces if part == 0 else contact + faces
        first_ref[pl.ds(part * SLABS, SLABS), :] = jnp.where(even, up, down)
        second_ref[pl.ds(part * SLABS, SLABS), :] = jnp.where(even, down, up)
    for out_ref in (first_ref, second_ref):
        out_ref[pl.ds(3 * SLABS, ROWS), :] = contact


def relax(differences, laplacian, values, base, rate, mix):
    e_xh, e_yh, e_zh = differences
    field_x = e_yh[2] - e_zh[1]
    field_y = e_zh[0] - e_xh[2]
    field_z = e_xh[1] - e_yh[0]
    saturation = rate * (field_x * field_x + field_y * field_y + field_z * field_z)
    reluctivity = base * (3.0 - 2.0 / (1.0 + saturation))
    updated = []
    for channel in range(4):
        total = reluctivity * laplacian[channel]
        for source in range(4):
            total = total + mix[channel][source] * values[source]
        updated.append(total)
    return updated


RING = 2 * ROWS
PAD = ROWS


def update_kernel(mix_hbm, owner_hbm, own_ref, inside_ref, across_ref, first_ref, second_ref, out_ref, *scratch):
    ring, cin, done, mix_ref, owner_ref, sems = scratch
    copies = [
        pltpu.make_async_copy(mix_hbm, mix_ref, sems.at[0]),
        pltpu.make_async_copy(owner_hbm, owner_ref, sems.at[1]),
    ]
    for copy in copies:
        copy.start()
    even_x = lax.axis_index("grp") % 2 == 0
    even_y = lax.axis_index("seg") % 2 == 0
    places = (1, jnp.where(even_x, 2, 0), jnp.where(even_x, 0, 2))
    row, lane = iotas()
    kz, yi, zi = row % BLZ, lane // BZC, lane % BZC
    first_half = row < BLZ
    up_lane = jnp.where(zi < BZC - 1, lane + 1, lane + 1 - BZC)
    down_lane = jnp.where(zi > 0, lane - 1, lane + BZC - 1)
    one = jnp.ones((ROWS, LANES), jnp.float32)
    zero = jnp.zeros((ROWS, LANES), jnp.float32)
    total = EXT * CH * RING

    def at(i, channel):
        return PAD + (i // BXC * SLABS + channel * BXC + i % BXC) * RING

    for now in range(2):
        ring[now, pl.ds(0, PAD), :] = zero
        ring[now, pl.ds(PAD + total, PAD), :] = zero
    for i, channel in ((0, 1), (0, 2), (0, 3), (0, 4), (BXC, 4)):
        ring[1, pl.ds(at(i, channel), ROWS), :] = zero
    for i, channel in ((BXC - 1, 5), (2 * BXC - 1, 5), (EXT - 1, 0), (EXT - 1, 1), (EXT - 1, 2)):
        ring[1, pl.ds(at(i, channel) + ROWS, ROWS), :] = zero
    for n, ref in enumerate((own_ref, inside_ref, across_ref)):
        part = places[n]
        begin = PAD + part * SLABS * RING
        if n > 0:
            begin = pl.multiple_of(begin, ROWS)
        for slab in range(SLABS):
            ring[0, pl.ds(begin + slab * RING + BLZ, ROWS), :] = ref[pl.ds(slab * ROWS, ROWS), :]
        first = first_ref[pl.ds(n * SLABS, SLABS), :]
        second = second_ref[pl.ds(n * SLABS, SLABS), :]
        compact_low = jnp.where(even_y, second, first)
        compact_high = jnp.where(even_y, first, second)
        wide_lane = lanes_of(SLABS)
        for k in range(BLZ):
            below = lroll(compact_low, LANES - (k + 1) * (LANES // 4))
            above = lroll(compact_high, -k * (LANES // 4))
            beyond = jnp.where(wide_lane >= LANES - LANES // 4, below, 0.0)
            beyond = jnp.where(wide_lane < LANES // 4, above, beyond)
            ring[0, pl.ds(begin + k, SLABS, stride=RING), :] = beyond
            ring[0, pl.ds(begin + k + 3 * BLZ, SLABS, stride=RING), :] = beyond
        contact = ref[pl.ds(FC, ROWS), :]
        first = first_ref[pl.ds(3 * SLABS, ROWS), :]
        second = second_ref[pl.ds(3 * SLABS, ROWS), :]
        faces = []
        beside = sroll(jnp.where(first_half == even_y, first, second), BLZ)
        for d in range(6):
            ab = jnp.broadcast_to(contact[:, d : d + 1], (ROWS, LANES))
            ba = sroll(ab, BLZ)
            at_lane = n * ROWS + d
            owners = jnp.broadcast_to(beside[:, at_lane : at_lane + 1], (ROWS, LANES))
            c = jnp.where(lane < LANES // 2, sroll(owners, BLZ), owners)
            ca = jnp.where(first_half, c, ba)
            bc = jnp.where(first_half, ba, sroll(c, BLZ))
            faces.append((ca, bc, ab))
        for g in range(3):
            f = [faces[d][g] for d in range(6)]
            ylow = jnp.where(yi == 0, f[2], one)
            yhigh = jnp.where(yi == BYC - 1, f[3], one)
            zlow = jnp.where(zi == 0, f[4], one)
            zlow_n = jnp.where(jnp.logical_and(zi == 0, kz == 0), 0.0, zlow)
            zhigh = jnp.where(zi == BZC - 1, f[5], one)
            zhigh_n = jnp.where(jnp.logical_and(zi == BZC - 1, kz == BLZ - 1), 0.0, zhigh)
            entries = (ylow, yhigh, zlow_n, zhigh, zhigh_n, ylow + zlow, f[0], f[1])
            for d, entry in enumerate(entries):
                cin[part, g, d] = entry

    def put(now, start, value):
        ring[now, pl.ds(start, ROWS), :] = value

    def sweep(now, i, last):
        part, x = i // BXC, i % BXC
        groups = (2,) if last else (0, 1)
        offset = {0: 0, 1: ROWS, 2: BLZ}
        coefs = {g: [cin[part, g, d] for d in range(8)] for g in groups}
        laps = {g: [] for g in groups}
        diffs = {g: ([], [], []) for g in groups}
        values = {g: [] for g in groups}
        for c in range(4):
            start, before, after = at(i, c), at(i - 1, c), at(i + 1, c)

            def tile(begin):
                return ring[now, pl.ds(begin, ROWS), :]

            rows = [tile(start + offset[g]) for g in range(3)]
            following, previous = {0: 2, 1: 0, 2: 1}, {0: 1, 1: 2, 2: 0}
            for g in groups:
                v = rows[g]
                cyl, cyh, nzl, czh, nzh, low, cxl, cxh = coefs[g]
                n_yh = lroll(jnp.where(yi == 0, rows[following[g]], v), -BZC)
                n_yl = lroll(jnp.where(yi == BYC - 1, rows[previous[g]], v), BZC)
                z_next = jnp.where(zi == 0, tile(start + offset[g] + 1), v)
                z_last = jnp.where(zi == BZC - 1, tile(start + offset[g] - 1), v)
                n_zh = jnp.take_along_axis(z_next, up_lane, axis=1)
                n_zl = jnp.take_along_axis(z_last, down_lane, axis=1)
                e_xl = v - tile(before + offset[g])
                if x == 0:
                    e_xl = cxl * e_xl
                e_xh = tile(after + offset[g]) - v
                if x == BXC - 1:
                    e_xh = cxh * e_xh
                e_yh = cyh * (n_yh - v)
                e_zh = nzh * n_zh - czh * v
                lap = (cyl * n_yl + nzl * n_zl) - low * v
                laps[g].append((lap - e_xl) + (e_xh + (e_yh + e_zh)))
                diffs[g][0].append(e_xh)
                diffs[g][1].append(e_yh)
                diffs[g][2].append(e_zh)
                values[g].append(v)
        for g in groups:
            base = ring[0, pl.ds(at(i, 4) + offset[g], ROWS), :] * step_size
            rate = ring[0, pl.ds(at(i, 5) + offset[g], ROWS), :]
            updated = relax(diffs[g], laps[g], values[g], base, rate, mix)
            if last:
                state[x] = updated
            else:
                for c in range(4):
                    put(1 - now, at(i, c) + offset[g], updated[c])

    for copy in copies:
        copy.wait()
    mix = [
        [step_size * mix_ref[c, e] + (1.0 if c == e else 0.0) for e in range(4)] for c in range(4)
    ]
    state = [None] * BXC
    for step in range(STEPS1):
        for i in range(step + 1, EXT - 1 - step):
            sweep(step % 2, i, step == STEPS1 - 1)

    y_inner = jnp.where(yi < BYC - 1, 1.0, 0.0)
    z_inner = jnp.where(zi < BZC - 1, 1.0, 0.0)
    y_low_inner = jnp.where(yi > 0, 1.0, 0.0)
    z_low_inner = jnp.where(zi > 0, 1.0, 0.0)
    out_ref[...] = jnp.zeros_like(out_ref)
    for _ in range(STEPS2):
        fresh = []
        rise = [[state[x + 1][c] - state[x][c] for c in range(4)] for x in range(BXC - 1)]
        rise.append([zero] * 4)
        for x in range(BXC):
            laps, diffs = [], ([], [], [])
            for c in range(4):
                v = state[x][c]
                e_yh = y_inner * (lroll(v, -BZC) - v)
                e_zh = z_inner * (lroll(v, -1) - v)
                e_yl = y_low_inner * (lroll(v, BZC) - v)
                e_zl = z_low_inner * (lroll(v, 1) - v)
                lap = (e_yl + e_yh) + (e_zl + e_zh)
                if x < BXC - 1:
                    lap = lap + rise[x][c]
                if x > 0:
                    lap = lap - rise[x - 1][c]
                laps.append(lap)
                diffs[0].append(rise[x][c])
                diffs[1].append(e_yh)
                diffs[2].append(e_zh)
            base = ring[0, pl.ds(at(BXC + x, 4) + BLZ, ROWS), :] * step_size
            rate = ring[0, pl.ds(at(BXC + x, 5) + BLZ, ROWS), :]
            fresh.append(relax(diffs, laps, state[x], base, rate, mix))
        state = fresh
    for x in range(BXC):
        for c in range(4):
            done[pl.ds((c * BXC + x) * ROWS, ROWS), :] = state[x][c]
    for block in range(ROWS):
        out_ref[owner_ref[0, block]] = done[pl.ds(block, 4 * BXC, stride=ROWS), :]


def on_device(initial_field, base_reluctivity, saturation_rate, mixing, face_contact, new_owner):
    f32 = jnp.float32
    cells = BLY * BYC
    peers = lax.axis_size("seg")
    small = pltpu.CompilerParams(vmem_limit_bytes=4 << 20)
    own = pl.pallas_call(
        pack_kernel,
        out_shape=jax.ShapeDtypeStruct((OWN, LANES), f32),
        in_specs=[HBM] * 4,
        out_specs=VMEM,
        scratch_shapes=[
            pltpu.VMEM((4 * BXC * cells, BLZ * BZC), f32),
            pltpu.VMEM((BXC * cells, BLZ * BZC), f32),
            pltpu.VMEM((BXC * cells, BLZ * BZC), f32),
            pltpu.SMEM((6, 1, ROWS), jnp.int32),
            pltpu.SemaphoreType.DMA((4,)),
        ],
        compiler_params=small,
        name="pack",
    )(
        in_hbm(initial_field.reshape(4 * BXC * cells, BLZ * BZC)),
        in_hbm(base_reluctivity.reshape(BXC * cells, BLZ * BZC)),
        in_hbm(saturation_rate.reshape(BXC * cells, BLZ * BZC)),
        in_hbm(face_contact.transpose(2, 0, 1)),
    )

    def swap(value, axis, offset):
        pairs = [(i, i + 1) for i in range(offset, lax.axis_size(axis) - 1, 2)]
        return lax.ppermute(value, axis, pairs + [(j, i) for i, j in pairs])

    inside = swap(own, "grp", 0)
    across = swap(own, "grp", 1)
    second, first = pl.pallas_call(
        edge_kernel,
        out_shape=(
            jax.ShapeDtypeStruct((EDGE, LANES), f32),
            jax.ShapeDtypeStruct((EDGE, LANES), f32),
        ),
        in_specs=[VMEM] * 3,
        out_specs=(VMEM, VMEM),
        compiler_params=small,
        name="edge",
    )(own, inside, across)
    first = swap(first, "seg", 0)
    second = swap(second, "seg", 1)
    placed = pl.pallas_call(
        update_kernel,
        out_shape=jax.ShapeDtypeStruct((peers, 4 * BXC, LANES), f32),
        in_specs=[ANY, ANY] + [VMEM] * 5,
        out_specs=VMEM,
        scratch_shapes=[
            pltpu.VMEM((2, EXT * CH * RING + 2 * PAD, LANES), f32),
            pltpu.VMEM((3, 3, 8, ROWS, LANES), f32),
            pltpu.VMEM((4 * BXC * ROWS, LANES), f32),
            pltpu.SMEM((4, 4), f32),
            pltpu.SMEM((1, BLY * BLZ), jnp.int32),
            pltpu.SemaphoreType.DMA((2,)),
        ],
        compiler_params=pltpu.CompilerParams(vmem_limit_bytes=8 << 20),
        name="update",
    )(mixing, new_owner, own, inside, across, first, second)
    received = lax.all_to_all(
        placed.reshape(peers, 4, BXC, LANES), "seg", split_axis=0, concat_axis=0, tiled=True
    )
    return received


def solution(mesh):
    return jax.shard_map(
        on_device,
        mesh=mesh,
        in_specs=(
            P(None, "grp", "seg", None),
            P("grp", "seg", None),
            P("grp", "seg", None),
            P(),
            P("grp", "seg", None),
            P("grp", "seg"),
        ),
        out_specs=P(("grp", "seg"), None, None, None),
        check_vma=False,
    )
```

```python
import jax
import jax.numpy as jnp
from jax import lax
from jax.experimental import pallas as pl
from jax.experimental.pallas import tpu as pltpu
from jax.sharding import PartitionSpec as P

BXC = 4
BYC = 16
BZC = 8
BLY = 2
BLZ = 4
STEPS1 = 4
STEPS2 = 4
ROWS = BLY * BLZ
LANES = BYC * BZC
CH = 6
SLABS = CH * BXC
FC = SLABS * ROWS
OWN = FC + ROWS
EDGE = 3 * SLABS + ROWS
EXT = 3 * BXC
step_size = 0.05

VMEM = pl.BlockSpec(memory_space=pltpu.VMEM)
SMEM = pl.BlockSpec(memory_space=pltpu.SMEM)
ANY = pl.BlockSpec(memory_space=pl.ANY)
HBM = pl.BlockSpec(memory_space=pltpu.HBM)


def in_hbm(value):
    return pltpu.with_memory_space_constraint(value, pltpu.HBM)


def iotas():
    row = lax.broadcasted_iota(jnp.int32, (ROWS, LANES), 0)
    lane = lax.broadcasted_iota(jnp.int32, (ROWS, LANES), 1)
    return row, lane


def lanes_of(rows):
    return lax.broadcasted_iota(jnp.int32, (rows, LANES), 1)


def lroll(value, shift):
    return value if shift % LANES == 0 else pltpu.roll(value, shift % LANES, 1)


def sroll(value, shift):
    return pltpu.roll(value, shift % ROWS, 0)


def pack_kernel(
    field_hbm,
    base_hbm,
    rate_hbm,
    contact_hbm,
    own_ref,
    field_ref,
    base_ref,
    rate_ref,
    contact_ref,
    sems,
):
    copies = [
        pltpu.make_async_copy(source, target, sems.at[n])
        for n, (source, target) in enumerate(
            (
                (contact_hbm, contact_ref),
                (base_hbm, base_ref),
                (rate_hbm, rate_ref),
                (field_hbm, field_ref),
            )
        )
    ]
    for copy in copies:
        copy.start()
    copies[0].wait()
    row, lane = iotas()
    contact = jnp.zeros((ROWS, LANES), jnp.float32)
    for d in range(6):
        for block in range(ROWS):
            here = jnp.logical_and(row == block, lane == d)
            contact = jnp.where(here, contact_ref[d, 0, block].astype(jnp.float32), contact)
    own_ref[pl.ds(FC, ROWS), :] = contact
    for copy in copies[1:]:
        copy.wait()
    first = 0
    for ref, slabs in ((field_ref, 4 * BXC), (base_ref, BXC), (rate_ref, BXC)):
        count = slabs * BLY
        group = lanes_of(count) // BZC % BLZ
        placed = [None] * BLZ
        for q in range(BLZ):
            mixed = jnp.concatenate(
                [ref[pl.ds(BLZ * r + q, count, stride=BYC), :] for r in range(BLZ)], axis=1
            )
            for kz in range(BLZ):
                moved = lroll(mixed, BZC * (q - kz))
                placed[kz] = moved if q == 0 else jnp.where(group == q, moved, placed[kz])
        for kz in range(BLZ):
            own_ref[pl.ds(first * ROWS + kz, count, stride=BLZ), :] = placed[kz]
        first += slabs


def edge_kernel(own_ref, inside_ref, across_ref, second_ref, first_ref):
    even = lax.axis_index("seg") % 2 == 0
    quarter = lanes_of(SLABS) // (LANES // 4)
    contact = None
    for part, ref in enumerate((own_ref, inside_ref, across_ref)):
        edges = []
        for jy, start in ((BLY - 1, LANES - LANES // 4), (0, 0)):
            edge = None
            for kz in range(BLZ):
                value = ref[pl.ds(jy * BLZ + kz, SLABS, stride=ROWS), :]
                moved = lroll(value, kz * (LANES // 4) - start)
                edge = moved if kz == 0 else jnp.where(quarter == kz, moved, edge)
            edges.append(edge)
        up, down = edges
        faces = lroll(ref[pl.ds(FC, ROWS), :], part * ROWS)
        contact = faces if part == 0 else contact + faces
        first_ref[pl.ds(part * SLABS, SLABS), :] = jnp.where(even, up, down)
        second_ref[pl.ds(part * SLABS, SLABS), :] = jnp.where(even, down, up)
    for out_ref in (first_ref, second_ref):
        out_ref[pl.ds(3 * SLABS, ROWS), :] = contact


def relax(differences, laplacian, values, base, rate, mix):
    e_xh, e_yh, e_zh = differences
    field_x = e_yh[2] - e_zh[1]
    field_y = e_zh[0] - e_xh[2]
    field_z = e_xh[1] - e_yh[0]
    saturation = rate * (field_x * field_x + field_y * field_y + field_z * field_z)
    reluctivity = base * (3.0 - 2.0 / (1.0 + saturation))
    updated = []
    for channel in range(4):
        total = reluctivity * laplacian[channel]
        for source in range(4):
            total = total + mix[channel][source] * values[source]
        updated.append(total)
    return updated


RING = 2 * ROWS
PAD = ROWS


def update_kernel(mix_hbm, owner_hbm, own_ref, inside_ref, across_ref, first_ref, second_ref, out_ref, *scratch):
    ring, cin, done, mix_ref, owner_ref, sems = scratch
    copies = [
        pltpu.make_async_copy(mix_hbm, mix_ref, sems.at[0]),
        pltpu.make_async_copy(owner_hbm, owner_ref, sems.at[1]),
    ]
    for copy in copies:
        copy.start()
    even_x = lax.axis_index("grp") % 2 == 0
    even_y = lax.axis_index("seg") % 2 == 0
    places = (1, jnp.where(even_x, 2, 0), jnp.where(even_x, 0, 2))
    row, lane = iotas()
    kz, yi, zi = row % BLZ, lane // BZC, lane % BZC
    first_half = row < BLZ
    up_lane = jnp.where(zi < BZC - 1, lane + 1, lane + 1 - BZC)
    down_lane = jnp.where(zi > 0, lane - 1, lane + BZC - 1)
    one = jnp.ones((ROWS, LANES), jnp.float32)
    zero = jnp.zeros((ROWS, LANES), jnp.float32)
    total = EXT * CH * RING

    def at(i, channel):
        return PAD + (i // BXC * SLABS + channel * BXC + i % BXC) * RING

    for now in range(2):
        ring[now, pl.ds(0, PAD), :] = zero
        ring[now, pl.ds(PAD + total, PAD), :] = zero
    above = [(0, 1), (0, 2), (0, 3), (0, 4), (BXC, 4)] + [(EXT - 2, c) for c in range(4)]
    for i, channel in above:
        ring[1, pl.ds(at(i, channel), ROWS), :] = zero
    below = [(BXC - 1, 5), (2 * BXC - 1, 5), (EXT - 1, 0), (EXT - 1, 1), (EXT - 1, 2)]
    for i, channel in below + [(1, c) for c in range(4)]:
        ring[1, pl.ds(at(i, channel) + ROWS, ROWS), :] = zero
    for n, ref in enumerate((own_ref, inside_ref, across_ref)):
        part = places[n]
        begin = PAD + part * SLABS * RING
        if n > 0:
            begin = pl.multiple_of(begin, ROWS)
        for slab in range(SLABS):
            ring[0, pl.ds(begin + slab * RING + BLZ, ROWS), :] = ref[pl.ds(slab * ROWS, ROWS), :]
        first = first_ref[pl.ds(n * SLABS, SLABS), :]
        second = second_ref[pl.ds(n * SLABS, SLABS), :]
        compact_low = jnp.where(even_y, second, first)
        compact_high = jnp.where(even_y, first, second)
        wide_lane = lanes_of(SLABS)
        for k in range(BLZ):
            below = lroll(compact_low, LANES - (k + 1) * (LANES // 4))
            above = lroll(compact_high, -k * (LANES // 4))
            beyond = jnp.where(wide_lane >= LANES - LANES // 4, below, 0.0)
            beyond = jnp.where(wide_lane < LANES // 4, above, beyond)
            ring[0, pl.ds(begin + k, SLABS, stride=RING), :] = beyond
            ring[0, pl.ds(begin + k + 3 * BLZ, SLABS, stride=RING), :] = beyond
        contact = ref[pl.ds(FC, ROWS), :]
        first = first_ref[pl.ds(3 * SLABS, ROWS), :]
        second = second_ref[pl.ds(3 * SLABS, ROWS), :]
        faces = []
        beside = sroll(jnp.where(first_half == even_y, first, second), BLZ)
        for d in range(6):
            ab = jnp.broadcast_to(contact[:, d : d + 1], (ROWS, LANES))
            ba = sroll(ab, BLZ)
            at_lane = n * ROWS + d
            owners = jnp.broadcast_to(beside[:, at_lane : at_lane + 1], (ROWS, LANES))
            c = jnp.where(lane < LANES // 2, sroll(owners, BLZ), owners)
            ca = jnp.where(first_half, c, ba)
            bc = jnp.where(first_half, ba, sroll(c, BLZ))
            faces.append((ca, bc, ab))
        for g in range(3):
            f = [faces[d][g] for d in range(6)]
            ylow = jnp.where(yi == 0, f[2], one)
            yhigh = jnp.where(yi == BYC - 1, f[3], one)
            zlow = jnp.where(zi == 0, f[4], one)
            zlow_n = jnp.where(jnp.logical_and(zi == 0, kz == 0), 0.0, zlow)
            zhigh = jnp.where(zi == BZC - 1, f[5], one)
            zhigh_n = jnp.where(jnp.logical_and(zi == BZC - 1, kz == BLZ - 1), 0.0, zhigh)
            entries = (ylow, yhigh, zlow_n, zhigh, zhigh_n, ylow + zlow, f[0], f[1])
            for d, entry in enumerate(entries):
                cin[part, g, d] = entry

    def put(now, start, value):
        ring[now, pl.ds(start, ROWS), :] = value

    def sweep(now, i, last, step):
        part, x = i // BXC, i % BXC
        alone = last or i in (step + 1, EXT - 2 - step)
        groups = (2,) if alone else (0, 1)
        offset = {0: 0, 1: ROWS, 2: BLZ}
        coefs = {g: [cin[part, g, d] for d in range(8)] for g in groups}
        laps = {g: [] for g in groups}
        diffs = {g: ([], [], []) for g in groups}
        values = {g: [] for g in groups}
        for c in range(4):
            start, before, after = at(i, c), at(i - 1, c), at(i + 1, c)

            def tile(begin):
                return ring[now, pl.ds(begin, ROWS), :]

            rows = [tile(start + offset[g]) for g in range(3)]
            following, previous = {0: 2, 1: 0, 2: 1}, {0: 1, 1: 2, 2: 0}
            for g in groups:
                v = rows[g]
                cyl, cyh, nzl, czh, nzh, low, cxl, cxh = coefs[g]
                n_yh = lroll(jnp.where(yi == 0, rows[following[g]], v), -BZC)
                n_yl = lroll(jnp.where(yi == BYC - 1, rows[previous[g]], v), BZC)
                z_next = jnp.where(zi == 0, tile(start + offset[g] + 1), v)
                z_last = jnp.where(zi == BZC - 1, tile(start + offset[g] - 1), v)
                n_zh = jnp.take_along_axis(z_next, up_lane, axis=1)
                n_zl = jnp.take_along_axis(z_last, down_lane, axis=1)
                e_xl = v - tile(before + offset[g])
                if x == 0:
                    e_xl = cxl * e_xl
                e_xh = tile(after + offset[g]) - v
                if x == BXC - 1:
                    e_xh = cxh * e_xh
                e_yh = cyh * (n_yh - v)
                e_zh = nzh * n_zh - czh * v
                lap = (cyl * n_yl + nzl * n_zl) - low * v
                laps[g].append((lap - e_xl) + (e_xh + (e_yh + e_zh)))
                diffs[g][0].append(e_xh)
                diffs[g][1].append(e_yh)
                diffs[g][2].append(e_zh)
                values[g].append(v)
        for g in groups:
            base = ring[0, pl.ds(at(i, 4) + offset[g], ROWS), :] * step_size
            rate = ring[0, pl.ds(at(i, 5) + offset[g], ROWS), :]
            updated = relax(diffs[g], laps[g], values[g], base, rate, mix)
            if last:
                state[x] = updated
            else:
                for c in range(4):
                    put(1 - now, at(i, c) + offset[g], updated[c])

    for copy in copies:
        copy.wait()
    mix = [
        [step_size * mix_ref[c, e] + (1.0 if c == e else 0.0) for e in range(4)] for c in range(4)
    ]
    state = [None] * BXC
    for step in range(STEPS1):
        for i in range(step + 1, EXT - 1 - step):
            sweep(step % 2, i, step == STEPS1 - 1, step)

    y_inner = jnp.where(yi < BYC - 1, 1.0, 0.0)
    z_inner = jnp.where(zi < BZC - 1, 1.0, 0.0)
    y_low_inner = jnp.where(yi > 0, 1.0, 0.0)
    z_low_inner = jnp.where(zi > 0, 1.0, 0.0)
    out_ref[...] = jnp.zeros_like(out_ref)
    for _ in range(STEPS2):
        fresh = []
        rise = [[state[x + 1][c] - state[x][c] for c in range(4)] for x in range(BXC - 1)]
        rise.append([zero] * 4)
        for x in range(BXC):
            laps, diffs = [], ([], [], [])
            for c in range(4):
                v = state[x][c]
                e_yh = y_inner * (lroll(v, -BZC) - v)
                e_zh = z_inner * (lroll(v, -1) - v)
                e_yl = y_low_inner * (lroll(v, BZC) - v)
                e_zl = z_low_inner * (lroll(v, 1) - v)
                lap = (e_yl + e_yh) + (e_zl + e_zh)
                if x < BXC - 1:
                    lap = lap + rise[x][c]
                if x > 0:
                    lap = lap - rise[x - 1][c]
                laps.append(lap)
                diffs[0].append(rise[x][c])
                diffs[1].append(e_yh)
                diffs[2].append(e_zh)
            base = ring[0, pl.ds(at(BXC + x, 4) + BLZ, ROWS), :] * step_size
            rate = ring[0, pl.ds(at(BXC + x, 5) + BLZ, ROWS), :]
            fresh.append(relax(diffs, laps, state[x], base, rate, mix))
        state = fresh
    for x in range(BXC):
        for c in range(4):
            done[pl.ds((c * BXC + x) * ROWS, ROWS), :] = state[x][c]
    for block in range(ROWS):
        out_ref[owner_ref[0, block]] = done[pl.ds(block, 4 * BXC, stride=ROWS), :]


def on_device(initial_field, base_reluctivity, saturation_rate, mixing, face_contact, new_owner):
    f32 = jnp.float32
    cells = BLY * BYC
    peers = lax.axis_size("seg")
    small = pltpu.CompilerParams(vmem_limit_bytes=4 << 20)
    own = pl.pallas_call(
        pack_kernel,
        out_shape=jax.ShapeDtypeStruct((OWN, LANES), f32),
        in_specs=[HBM] * 4,
        out_specs=VMEM,
        scratch_shapes=[
            pltpu.VMEM((4 * BXC * cells, BLZ * BZC), f32),
            pltpu.VMEM((BXC * cells, BLZ * BZC), f32),
            pltpu.VMEM((BXC * cells, BLZ * BZC), f32),
            pltpu.SMEM((6, 1, ROWS), jnp.int32),
            pltpu.SemaphoreType.DMA((4,)),
        ],
        compiler_params=small,
        name="pack",
    )(
        in_hbm(initial_field.reshape(4 * BXC * cells, BLZ * BZC)),
        in_hbm(base_reluctivity.reshape(BXC * cells, BLZ * BZC)),
        in_hbm(saturation_rate.reshape(BXC * cells, BLZ * BZC)),
        in_hbm(face_contact.transpose(2, 0, 1)),
    )

    def swap(value, axis, offset):
        pairs = [(i, i + 1) for i in range(offset, lax.axis_size(axis) - 1, 2)]
        return lax.ppermute(value, axis, pairs + [(j, i) for i, j in pairs])

    inside = swap(own, "grp", 0)
    across = swap(own, "grp", 1)
    second, first = pl.pallas_call(
        edge_kernel,
        out_shape=(
            jax.ShapeDtypeStruct((EDGE, LANES), f32),
            jax.ShapeDtypeStruct((EDGE, LANES), f32),
        ),
        in_specs=[VMEM] * 3,
        out_specs=(VMEM, VMEM),
        compiler_params=small,
        name="edge",
    )(own, inside, across)
    first = swap(first, "seg", 0)
    second = swap(second, "seg", 1)
    placed = pl.pallas_call(
        update_kernel,
        out_shape=jax.ShapeDtypeStruct((peers, 4 * BXC, LANES), f32),
        in_specs=[ANY, ANY] + [VMEM] * 5,
        out_specs=VMEM,
        scratch_shapes=[
            pltpu.VMEM((2, EXT * CH * RING + 2 * PAD, LANES), f32),
            pltpu.VMEM((3, 3, 8, ROWS, LANES), f32),
            pltpu.VMEM((4 * BXC * ROWS, LANES), f32),
            pltpu.SMEM((4, 4), f32),
            pltpu.SMEM((1, BLY * BLZ), jnp.int32),
            pltpu.SemaphoreType.DMA((2,)),
        ],
        compiler_params=pltpu.CompilerParams(vmem_limit_bytes=8 << 20),
        name="update",
    )(mixing, new_owner, own, inside, across, first, second)
    received = lax.all_to_all(
        placed.reshape(peers, 4, BXC, LANES), "seg", split_axis=0, concat_axis=0, tiled=True
    )
    return received


def solution(mesh):
    return jax.shard_map(
        on_device,
        mesh=mesh,
        in_specs=(
            P(None, "grp", "seg", None),
            P("grp", "seg", None),
            P("grp", "seg", None),
            P(),
            P("grp", "seg", None),
            P("grp", "seg"),
        ),
        out_specs=P(("grp", "seg"), None, None, None),
        check_vma=False,
    )
```

```python
import jax
import jax.numpy as jnp
from jax import lax
from jax.experimental import pallas as pl
from jax.experimental.pallas import tpu as pltpu
from jax.sharding import PartitionSpec as P

BXC = 4
BYC = 16
BZC = 8
BLY = 2
BLZ = 4
STEPS1 = 4
STEPS2 = 4
ROWS = BLY * BLZ
LANES = BYC * BZC
CH = 6
SLABS = CH * BXC
FC = SLABS * ROWS
OWN = FC + ROWS
EDGE = 3 * SLABS + ROWS
EXT = 3 * BXC
step_size = 0.05

VMEM = pl.BlockSpec(memory_space=pltpu.VMEM)
SMEM = pl.BlockSpec(memory_space=pltpu.SMEM)
ANY = pl.BlockSpec(memory_space=pl.ANY)
HBM = pl.BlockSpec(memory_space=pltpu.HBM)


def in_hbm(value):
    return pltpu.with_memory_space_constraint(value, pltpu.HBM)


def iotas():
    row = lax.broadcasted_iota(jnp.int32, (ROWS, LANES), 0)
    lane = lax.broadcasted_iota(jnp.int32, (ROWS, LANES), 1)
    return row, lane


def lanes_of(rows):
    return lax.broadcasted_iota(jnp.int32, (rows, LANES), 1)


def lroll(value, shift):
    return value if shift % LANES == 0 else pltpu.roll(value, shift % LANES, 1)


def sroll(value, shift):
    return pltpu.roll(value, shift % ROWS, 0)


def pack_kernel(
    field_hbm,
    base_hbm,
    rate_hbm,
    contact_hbm,
    own_ref,
    field_ref,
    base_ref,
    rate_ref,
    contact_ref,
    sems,
):
    copies = [
        pltpu.make_async_copy(source, target, sems.at[n])
        for n, (source, target) in enumerate(
            (
                (contact_hbm, contact_ref),
                (base_hbm, base_ref),
                (rate_hbm, rate_ref),
                (field_hbm, field_ref),
            )
        )
    ]
    for copy in copies:
        copy.start()
    copies[0].wait()
    row, lane = iotas()
    contact = jnp.zeros((ROWS, LANES), jnp.float32)
    for d in range(6):
        for block in range(ROWS):
            here = jnp.logical_and(row == block, lane == d)
            contact = jnp.where(here, contact_ref[d, 0, block].astype(jnp.float32), contact)
    own_ref[pl.ds(FC, ROWS), :] = contact
    for copy in copies[1:]:
        copy.wait()
    first = 0
    for ref, slabs in ((field_ref, 4 * BXC), (base_ref, BXC), (rate_ref, BXC)):
        count = slabs * BLY
        group = lanes_of(count) // BZC % BLZ
        placed = [None] * BLZ
        for q in range(BLZ):
            mixed = jnp.concatenate(
                [ref[pl.ds(BLZ * r + q, count, stride=BYC), :] for r in range(BLZ)], axis=1
            )
            for kz in range(BLZ):
                moved = lroll(mixed, BZC * (q - kz))
                placed[kz] = moved if q == 0 else jnp.where(group == q, moved, placed[kz])
        for kz in range(BLZ):
            own_ref[pl.ds(first * ROWS + kz, count, stride=BLZ), :] = placed[kz]
        first += slabs


def edge_kernel(own_ref, inside_ref, across_ref, second_ref, first_ref):
    even = lax.axis_index("seg") % 2 == 0
    quarter = lanes_of(SLABS) // (LANES // 4)
    contact = None
    for part, ref in enumerate((own_ref, inside_ref, across_ref)):
        edges = []
        for jy, start in ((BLY - 1, LANES - LANES // 4), (0, 0)):
            edge = None
            for kz in range(BLZ):
                value = ref[pl.ds(jy * BLZ + kz, SLABS, stride=ROWS), :]
                moved = lroll(value, kz * (LANES // 4) - start)
                edge = moved if kz == 0 else jnp.where(quarter == kz, moved, edge)
            edges.append(edge)
        up, down = edges
        faces = lroll(ref[pl.ds(FC, ROWS), :], part * ROWS)
        contact = faces if part == 0 else contact + faces
        first_ref[pl.ds(part * SLABS, SLABS), :] = jnp.where(even, up, down)
        second_ref[pl.ds(part * SLABS, SLABS), :] = jnp.where(even, down, up)
    for out_ref in (first_ref, second_ref):
        out_ref[pl.ds(3 * SLABS, ROWS), :] = contact


def relax(differences, laplacian, values, base, rate, mix):
    e_xh, e_yh, e_zh = differences
    field_x = e_yh[2] - e_zh[1]
    field_y = e_zh[0] - e_xh[2]
    field_z = e_xh[1] - e_yh[0]
    saturation = rate * (field_x * field_x + field_y * field_y + field_z * field_z)
    reluctivity = base * (3.0 - 2.0 / (1.0 + saturation))
    updated = []
    for channel in range(4):
        total = reluctivity * laplacian[channel]
        for source in range(4):
            total = total + mix[channel][source] * values[source]
        updated.append(total)
    return updated


RING = 2 * ROWS
PAD = ROWS


def update_kernel(mix_hbm, owner_hbm, own_ref, inside_ref, across_ref, first_ref, second_ref, out_ref, *scratch):
    ring, cin, done, mix_ref, owner_ref, sems = scratch
    copies = [
        pltpu.make_async_copy(mix_hbm, mix_ref, sems.at[0]),
        pltpu.make_async_copy(owner_hbm, owner_ref, sems.at[1]),
    ]
    for copy in copies:
        copy.start()
    even_x = lax.axis_index("grp") % 2 == 0
    even_y = lax.axis_index("seg") % 2 == 0
    places = (1, jnp.where(even_x, 2, 0), jnp.where(even_x, 0, 2))
    row, lane = iotas()
    kz, yi, zi = row % BLZ, lane // BZC, lane % BZC
    first_half = row < BLZ
    up_lane = jnp.where(zi < BZC - 1, lane + 1, lane + 1 - BZC)
    down_lane = jnp.where(zi > 0, lane - 1, lane + BZC - 1)
    one = jnp.ones((ROWS, LANES), jnp.float32)
    zero = jnp.zeros((ROWS, LANES), jnp.float32)
    total = EXT * CH * RING

    def at(i, channel):
        return PAD + (i // BXC * SLABS + channel * BXC + i % BXC) * RING

    for now in range(2):
        ring[now, pl.ds(0, PAD), :] = zero
        ring[now, pl.ds(PAD + total, PAD), :] = zero
    above = [(0, 1), (0, 2), (0, 3), (0, 4), (BXC, 4)] + [(EXT - 2, c) for c in range(4)]
    for i, channel in above:
        ring[1, pl.ds(at(i, channel), ROWS), :] = zero
    below = [(BXC - 1, 5), (2 * BXC - 1, 5), (EXT - 1, 0), (EXT - 1, 1), (EXT - 1, 2)]
    for i, channel in below + [(1, c) for c in range(4)]:
        ring[1, pl.ds(at(i, channel) + ROWS, ROWS), :] = zero
    for n, ref in enumerate((own_ref, inside_ref, across_ref)):
        part = places[n]
        begin = PAD + part * SLABS * RING
        if n > 0:
            begin = pl.multiple_of(begin, ROWS)
        for slab in range(SLABS):
            ring[0, pl.ds(begin + slab * RING + BLZ, ROWS), :] = ref[pl.ds(slab * ROWS, ROWS), :]
        first = first_ref[pl.ds(n * SLABS, SLABS), :]
        second = second_ref[pl.ds(n * SLABS, SLABS), :]
        compact_low = jnp.where(even_y, second, first)
        compact_high = jnp.where(even_y, first, second)
        wide_lane = lanes_of(SLABS)
        for k in range(BLZ):
            below = lroll(compact_low, LANES - (k + 1) * (LANES // 4))
            above = lroll(compact_high, -k * (LANES // 4))
            beyond = jnp.where(wide_lane >= LANES - LANES // 4, below, 0.0)
            beyond = jnp.where(wide_lane < LANES // 4, above, beyond)
            ring[0, pl.ds(begin + k, SLABS, stride=RING), :] = beyond
            ring[0, pl.ds(begin + k + 3 * BLZ, SLABS, stride=RING), :] = beyond
        contact = ref[pl.ds(FC, ROWS), :]
        first = first_ref[pl.ds(3 * SLABS, ROWS), :]
        second = second_ref[pl.ds(3 * SLABS, ROWS), :]
        faces = []
        beside = sroll(jnp.where(first_half == even_y, first, second), BLZ)
        for d in range(6):
            ab = jnp.broadcast_to(contact[:, d : d + 1], (ROWS, LANES))
            ba = sroll(ab, BLZ)
            at_lane = n * ROWS + d
            owners = jnp.broadcast_to(beside[:, at_lane : at_lane + 1], (ROWS, LANES))
            c = jnp.where(lane < LANES // 2, sroll(owners, BLZ), owners)
            ca = jnp.where(first_half, c, ba)
            bc = jnp.where(first_half, ba, sroll(c, BLZ))
            faces.append((ca, bc, ab))
        for g in range(3):
            f = [faces[d][g] for d in range(6)]
            ylow = jnp.where(yi == 0, f[2], one)
            yhigh = jnp.where(yi == BYC - 1, f[3], one)
            zlow = jnp.where(zi == 0, f[4], one)
            zlow_n = jnp.where(jnp.logical_and(zi == 0, kz == 0), 0.0, zlow)
            zhigh = jnp.where(zi == BZC - 1, f[5], one)
            zhigh_n = jnp.where(jnp.logical_and(zi == BZC - 1, kz == BLZ - 1), 0.0, zhigh)
            entries = (ylow, yhigh, zlow_n, zhigh, zhigh_n, ylow + zlow, f[0], f[1])
            for d, entry in enumerate(entries):
                cin[part, g, d] = entry

    def put(now, start, value):
        ring[now, pl.ds(start, ROWS), :] = value

    def sweep(now, i, last, step):
        part, x = i // BXC, i % BXC
        alone = last or i in (step + 1, EXT - 2 - step)
        groups = (2,) if alone else (0, 1)
        offset = {0: 0, 1: ROWS, 2: BLZ}
        coefs = {g: [cin[part, g, d] for d in range(8)] for g in groups}
        laps = {g: [] for g in groups}
        diffs = {g: ([], [], []) for g in groups}
        values = {g: [] for g in groups}
        for c in range(4):
            start, before, after = at(i, c), at(i - 1, c), at(i + 1, c)

            def tile(begin):
                return ring[now, pl.ds(begin, ROWS), :]

            rows = [tile(start + offset[g]) for g in range(3)]
            following, previous = {0: 2, 1: 0, 2: 1}, {0: 1, 1: 2, 2: 0}
            for g in groups:
                v = rows[g]
                cyl, cyh, nzl, czh, nzh, low, cxl, cxh = coefs[g]
                n_yh = lroll(jnp.where(yi == 0, rows[following[g]], v), -BZC)
                n_yl = lroll(jnp.where(yi == BYC - 1, rows[previous[g]], v), BZC)
                z_next = jnp.where(zi == 0, tile(start + offset[g] + 1), v)
                z_last = jnp.where(zi == BZC - 1, tile(start + offset[g] - 1), v)
                n_zh = jnp.take_along_axis(z_next, up_lane, axis=1)
                n_zl = jnp.take_along_axis(z_last, down_lane, axis=1)
                e_xl = v - tile(before + offset[g])
                if x == 0:
                    e_xl = cxl * e_xl
                e_xh = tile(after + offset[g]) - v
                if x == BXC - 1:
                    e_xh = cxh * e_xh
                e_yh = cyh * (n_yh - v)
                e_zh = nzh * n_zh - czh * v
                lap = (cyl * n_yl + nzl * n_zl) - low * v
                laps[g].append((lap - e_xl) + (e_xh + (e_yh + e_zh)))
                diffs[g][0].append(e_xh)
                diffs[g][1].append(e_yh)
                diffs[g][2].append(e_zh)
                values[g].append(v)
        for g in groups:
            base = ring[0, pl.ds(at(i, 4) + offset[g], ROWS), :] * step_size
            rate = ring[0, pl.ds(at(i, 5) + offset[g], ROWS), :]
            updated = relax(diffs[g], laps[g], values[g], base, rate, mix)
            if last:
                state[x] = updated
            else:
                for c in range(4):
                    put(1 - now, at(i, c) + offset[g], updated[c])

    for copy in copies:
        copy.wait()
    mix = [
        [step_size * mix_ref[c, e] + (1.0 if c == e else 0.0) for e in range(4)] for c in range(4)
    ]
    state = [None] * BXC
    for step in range(STEPS1):
        for i in range(step + 1, EXT - 1 - step):
            sweep(step % 2, i, step == STEPS1 - 1, step)

    y_inner = jnp.where(yi < BYC - 1, 1.0, 0.0)
    z_inner = jnp.where(zi < BZC - 1, 1.0, 0.0)
    y_low_inner = jnp.where(yi > 0, 1.0, 0.0)
    z_low_inner = jnp.where(zi > 0, 1.0, 0.0)
    out_ref[...] = jnp.zeros_like(out_ref)

    def settle(_, state):
        fresh = []
        rise = [[state[x + 1][c] - state[x][c] for c in range(4)] for x in range(BXC - 1)]
        rise.append([zero] * 4)
        for x in range(BXC):
            laps, diffs = [], ([], [], [])
            for c in range(4):
                v = state[x][c]
                e_yh = y_inner * (lroll(v, -BZC) - v)
                e_zh = z_inner * (lroll(v, -1) - v)
                e_yl = y_low_inner * (lroll(v, BZC) - v)
                e_zl = z_low_inner * (lroll(v, 1) - v)
                lap = (e_yl + e_yh) + (e_zl + e_zh)
                if x < BXC - 1:
                    lap = lap + rise[x][c]
                if x > 0:
                    lap = lap - rise[x - 1][c]
                laps.append(lap)
                diffs[0].append(rise[x][c])
                diffs[1].append(e_yh)
                diffs[2].append(e_zh)
            base = ring[0, pl.ds(at(BXC + x, 4) + BLZ, ROWS), :] * step_size
            rate = ring[0, pl.ds(at(BXC + x, 5) + BLZ, ROWS), :]
            fresh.append(relax(diffs, laps, state[x], base, rate, mix))
        return fresh

    state = lax.fori_loop(0, STEPS2, settle, state)
    for x in range(BXC):
        for c in range(4):
            done[pl.ds((c * BXC + x) * ROWS, ROWS), :] = state[x][c]
    for block in range(ROWS):
        out_ref[owner_ref[0, block]] = done[pl.ds(block, 4 * BXC, stride=ROWS), :]


def on_device(initial_field, base_reluctivity, saturation_rate, mixing, face_contact, new_owner):
    f32 = jnp.float32
    cells = BLY * BYC
    peers = lax.axis_size("seg")
    small = pltpu.CompilerParams(vmem_limit_bytes=4 << 20)
    own = pl.pallas_call(
        pack_kernel,
        out_shape=jax.ShapeDtypeStruct((OWN, LANES), f32),
        in_specs=[HBM] * 4,
        out_specs=VMEM,
        scratch_shapes=[
            pltpu.VMEM((4 * BXC * cells, BLZ * BZC), f32),
            pltpu.VMEM((BXC * cells, BLZ * BZC), f32),
            pltpu.VMEM((BXC * cells, BLZ * BZC), f32),
            pltpu.SMEM((6, 1, ROWS), jnp.int32),
            pltpu.SemaphoreType.DMA((4,)),
        ],
        compiler_params=small,
        name="pack",
    )(
        in_hbm(initial_field.reshape(4 * BXC * cells, BLZ * BZC)),
        in_hbm(base_reluctivity.reshape(BXC * cells, BLZ * BZC)),
        in_hbm(saturation_rate.reshape(BXC * cells, BLZ * BZC)),
        in_hbm(face_contact.transpose(2, 0, 1)),
    )

    def swap(value, axis, offset):
        pairs = [(i, i + 1) for i in range(offset, lax.axis_size(axis) - 1, 2)]
        return lax.ppermute(value, axis, pairs + [(j, i) for i, j in pairs])

    inside = swap(own, "grp", 0)
    across = swap(own, "grp", 1)
    second, first = pl.pallas_call(
        edge_kernel,
        out_shape=(
            jax.ShapeDtypeStruct((EDGE, LANES), f32),
            jax.ShapeDtypeStruct((EDGE, LANES), f32),
        ),
        in_specs=[VMEM] * 3,
        out_specs=(VMEM, VMEM),
        compiler_params=small,
        name="edge",
    )(own, inside, across)
    first = swap(first, "seg", 0)
    second = swap(second, "seg", 1)
    placed = pl.pallas_call(
        update_kernel,
        out_shape=jax.ShapeDtypeStruct((peers, 4 * BXC, LANES), f32),
        in_specs=[ANY, ANY] + [VMEM] * 5,
        out_specs=VMEM,
        scratch_shapes=[
            pltpu.VMEM((2, EXT * CH * RING + 2 * PAD, LANES), f32),
            pltpu.VMEM((3, 3, 8, ROWS, LANES), f32),
            pltpu.VMEM((4 * BXC * ROWS, LANES), f32),
            pltpu.SMEM((4, 4), f32),
            pltpu.SMEM((1, BLY * BLZ), jnp.int32),
            pltpu.SemaphoreType.DMA((2,)),
        ],
        compiler_params=pltpu.CompilerParams(vmem_limit_bytes=8 << 20),
        name="update",
    )(mixing, new_owner, own, inside, across, first, second)
    received = lax.all_to_all(
        placed.reshape(peers, 4, BXC, LANES), "seg", split_axis=0, concat_axis=0, tiled=True
    )
    return received


def solution(mesh):
    return jax.shard_map(
        on_device,
        mesh=mesh,
        in_specs=(
            P(None, "grp", "seg", None),
            P("grp", "seg", None),
            P("grp", "seg", None),
            P(),
            P("grp", "seg", None),
            P("grp", "seg"),
        ),
        out_specs=P(("grp", "seg"), None, None, None),
        check_vma=False,
    )
```
